32 devices in a mesh: group: 2 (over y), ctx: 4 (over z), head: 4 (over x, core).
Axes of the slice: x: 2, y: 2, z: 4, core: 2. Of those that a mesh axis runs over, the one named last changes fastest.
Arguments:
- query: bfloat16 [1024, 4096], P(('group', 'ctx'), 'head'), parts along dimension 0, may hold values from -8 to 8
- keys: bfloat16 [1024, 512], P(('group', 'ctx'), 'head'), parts along dimension 0, may hold values from -6 to 6
- values: bfloat16 [1024, 512], P(('group', 'ctx'), 'head'), parts along dimension 0, may hold values from -6 to 6
- residual: bfloat16 [1024, 2048], P(('group', 'ctx', 'head')), parts along dimension 0, may hold values from -15 to 15
- o_weight: bfloat16 [4096, 2048], P('head', 'ctx'), may hold values from -0.09375 to 0.09375
- gain: float32 [2048], replicated, may hold values from 0.1 to 1.9
- routes: int32 [1024, 8], P(('group', 'ctx', 'head')), parts along dimension 0, may hold values from 0 to 15, all different within a row; in each aligned block of 32 rows (0 to 31, 32 to 63, ...) at most 32 rows name the same one
- gates: float32 [1024, 8], P(('group', 'ctx', 'head')), parts along dimension 0, may hold values from 0.05 to 1
- w_gate: bfloat16 [16, 2048, 768], P(('ctx', 'head')), may hold values from -0.125 to 0.125
- w_up: bfloat16 [16, 2048, 768], P(('ctx', 'head')), may hold values from -0.125 to 0.125
- w_down: bfloat16 [16, 768, 2048], P(('ctx', 'head')), may hold values from -0.625 to 0.625
Outputs:
- mixed: bfloat16 [1024, 2048], P(('group', 'ctx', 'head')), parts along dimension 0
- expert_mix: bfloat16 [1024, 2048], P(('group', 'ctx', 'head')), parts along dimension 0
The draws below stay inside these ranges and needn't reach their ends.
There are 2 independent parts, one for each index of `group`. The reference program is written for one: setup_inputs(seed, part) draws one part's arguments, and reference() takes and returns one part's arrays. A program takes and returns all parts, laid end to end along the dimension named above; an argument that names none is the same for every part. Nothing has to cross between parts.
Inputs may be any that keep to these rules, and one draw needn't show every extreme that they name: `routes`: the 8 experts of a token are distinct. In each aligned block of 32 tokens (the tokens of one owner device), no expert is named more than 32 times, a bound that some block reaches.
All inputs are finite; a program needn't handle non-finite values.
Results may differ from the reference program's by a relative error of at most 0.019.
Values may be sent and summed in bfloat16 or wider, within the bound.
No kernel may reach another device: no remote copies, remote signals or barrier semaphores. Data moves between devices by JAX's collectives and lax.ppermute only.
A program may use at most 128 MiB of HBM per device.

```python
import math
import jax
import jax.numpy as jnp
import numpy as np
from jax import lax

D = 2048
QUERY_HEADS = 32
KEY_VALUE_HEADS = 4
HEAD_DIMENSION = 128
FE = 768
TOPK = 8
PROMPT_TOKENS = 512
TOK_OWN = 32
EXPERTS = 16
CAP = 32
N_CTX = 4
N_HEAD = 4


def draw_query(key, part):
    random_seed_key = jax.random.fold_in(key, 11)
    return jnp.clip(2.5 * jax.random.normal(random_seed_key, (PROMPT_TOKENS, QUERY_HEADS * HEAD_DIMENSION), jnp.float32), -8.0, 8.0).astype(jnp.bfloat16)


def draw_keys(key, part):
    random_seed_key = jax.random.fold_in(key, 23)
    return jnp.clip(jax.random.normal(random_seed_key, (PROMPT_TOKENS, KEY_VALUE_HEADS * HEAD_DIMENSION), jnp.float32), -6.0, 6.0).astype(jnp.bfloat16)


def draw_residual(key, part):
    row_key = jax.random.fold_in(key, 31)
    col_key = jax.random.fold_in(key, 37)
    random_seed_key = jax.random.fold_in(key, 41)
    row_scale = jnp.exp(jax.random.uniform(row_key, (PROMPT_TOKENS, 1), jnp.float32, jnp.log(0.3), jnp.log(1.5)))
    col_scale = jnp.exp(jax.random.uniform(col_key, (1, D), jnp.float32, jnp.log(0.25), jnp.log(2.5)))
    random_field = jnp.clip(jax.random.normal(random_seed_key, (PROMPT_TOKENS, D), jnp.float32), -4.0, 4.0)
    return (random_field * row_scale * col_scale).astype(jnp.bfloat16)


def block_levels(stream_key, shape, split, least, largest):
    factor_of, own = 1.0, jax.random.fold_in(stream_key, 6)
    for axis_at, blocks in split:
        steps = jnp.exp(jax.random.uniform(jax.random.fold_in(own, axis_at), (blocks,), jnp.float32, least / len(split), largest / len(split)))
        factor_of = factor_of * jnp.repeat(steps, shape[axis_at] // blocks).reshape([-1 if axis == axis_at else 1 for axis in range(len(shape))])
    return factor_of


def shared_out(own_key, own, number, rows, number_of, top, limit, skew):
    ranking = jax.random.permutation(own_key, number_of)
    heavy_load, usual = portions_of(number_of, rows * top, limit, skew, True), portions_of(number_of, rows * top, limit, skew, False)
    places = jnp.arange(number_of)

    def named(sizes, turn):
        used = int((sizes > 0).sum())
        fixed = max(1, used // 4)
        moved = fixed + (places - fixed + turn * (used - fixed)) % max(1, number_of - fixed)
        return jnp.zeros((number_of,), jnp.int32).at[ranking[jnp.where(places < fixed, places, moved)]].set(jnp.asarray(sizes, jnp.int32))

    sizes = jnp.where(number % 4 == 0, named(heavy_load, number // 4), named(usual, number - number // 4 - 1))
    mixed = jax.random.permutation(jax.random.fold_in(own, 3), number_of)
    giver, sink = mixed[0:number_of // 2 * 2:2], mixed[1:number_of // 2 * 2:2]
    margin = jnp.minimum(sizes[giver] - 1, limit - sizes[sink]) // 2
    margin = jnp.where((giver == ranking[0]) | (sink == ranking[0]) | (sizes[sink] == 0), 0, jnp.maximum(margin, 0))
    moved = jax.random.randint(jax.random.fold_in(own, 4), (number_of // 2,), 0, 1 << 20) % (margin + 1)
    sizes = sizes.at[giver].add(-moved).at[sink].add(moved)
    labels = jnp.searchsorted(jnp.cumsum(sizes), jnp.arange(rows * top), side="right").astype(jnp.int32)
    listing = labels.reshape(top, rows).T
    listing = listing[jax.random.permutation(jax.random.fold_in(own, 1), rows)]
    turn = jax.random.randint(jax.random.fold_in(own, 2), (rows, 1), 0, top)
    return jnp.take_along_axis(listing, (jnp.arange(top)[None, :] + turn) % top, axis=1)


def portions_of(number_of, total, limit, slope, full):
    portions = [(1 << 20) // math.isqrt(grade ** slope) + 1 for grade in range(1, number_of + 1)]
    largest = limit if full else min(limit, max(-(-total // number_of), total * portions[0] // sum(portions)))
    least = 1 if total - largest >= number_of - 1 else 0
    holding, spare = [largest] + [least] * (number_of - 1), total - largest - least * (number_of - 1)
    while spare > 0:
        movable = [i for i in range(1, number_of) if holding[i] < largest] or [i for i in range(1, number_of) if holding[i] < limit]
        mass, budget = sum([portions[i] for i in movable]), spare
        for i in movable:
            extra = min(limit - holding[i], max(1, budget * portions[i] // mass), spare)
            holding[i] = holding[i] + extra
            spare = spare - extra
    return np.array(holding)


def noise(own_key, shape, scale, limit, pieces=(), kind=jnp.bfloat16):
    drawn = scale * jax.random.normal(own_key, shape, jnp.float32)
    if pieces:
        drawn = drawn * block_levels(own_key, shape, pieces, -0.22, 0.18)
    return jnp.clip(drawn, -limit, limit).astype(kind)


def setup_inputs(seed: int = 0, part: int = 0) -> dict:
    key_of = jax.random.split(jax.random.key(seed), 12)
    part_splits = jax.random.split(jax.random.fold_in(key_of[11], part), 12)
    query = draw_query(jax.random.fold_in(jax.random.fold_in(key_of[11], part), 71), part)
    keys = draw_keys(jax.random.fold_in(jax.random.fold_in(key_of[11], part), 71), part)
    values = noise(part_splits[2], (PROMPT_TOKENS, KEY_VALUE_HEADS * HEAD_DIMENSION), 1.0, 6.0, ((0, 4), (1, 4)))
    residual = draw_residual(jax.random.fold_in(jax.random.fold_in(key_of[11], part), 71), part)
    o_weight = noise(key_of[4], (QUERY_HEADS * HEAD_DIMENSION, D), (QUERY_HEADS * HEAD_DIMENSION) ** -0.5, 0.09375, ((0, 4), (1, 4)))
    gain = jnp.clip(1.0 + 0.18 * jax.random.normal(key_of[5], (D,), jnp.float32), 0.1, 1.9)
    routes_keys = jax.random.split(jax.random.fold_in(part_splits[6], 1), PROMPT_TOKENS // TOK_OWN)
    routes_turns = jax.random.permutation(jax.random.fold_in(part_splits[6], 3), PROMPT_TOKENS // TOK_OWN)
    routes = jax.vmap(lambda own, number: shared_out(jax.random.fold_in(part_splits[6], 2), own, number, TOK_OWN, EXPERTS, TOPK, CAP, 2))(routes_keys, routes_turns).reshape((PROMPT_TOKENS, TOPK))
    gates = jnp.clip(jnp.exp(math.log(1.0) - 2.9957323 * jax.random.uniform(part_splits[7], (PROMPT_TOKENS, TOPK), jnp.float32) ** block_levels(part_splits[7], (PROMPT_TOKENS, TOPK), ((0, 16),), -0.2, 0.2)), 0.05, 1.0)
    w_gate = noise(key_of[8], (EXPERTS, D, FE), D ** -0.5, 0.125, ((0, 16),))
    w_up = noise(key_of[9], (EXPERTS, D, FE), D ** -0.5, 0.125, ((0, 16),))
    w_down = noise(key_of[10], (EXPERTS, FE, D), (FE // 8) ** -0.5, 0.625, ((0, 16),))
    return dict(query=query, keys=keys, values=values, residual=residual, o_weight=o_weight, gain=gain, routes=routes, gates=gates, w_gate=w_gate, w_up=w_up, w_down=w_down)


def attend_one(operands):
    q_head, k_head, v_head = operands
    positions = jnp.arange(PROMPT_TOKENS, dtype=jnp.int32)
    causal = positions[None, :] <= positions[:, None]
    scores = jnp.dot(q_head, k_head.T, preferred_element_type=jnp.float32) * HEAD_DIMENSION ** (-0.5)
    scores = jnp.where(causal, scores, -1e+30)
    row_max = lax.optimization_barrier(jnp.max(scores, axis=-1, keepdims=True))
    expw = jnp.where(causal, jnp.exp(scores - row_max), 0.0)
    total = lax.optimization_barrier(jnp.sum(expw, axis=-1, keepdims=True))
    summed = jnp.dot(expw.astype(jnp.bfloat16), v_head, preferred_element_type=jnp.float32)
    return (summed / total).astype(jnp.bfloat16)

def reference(query, keys, values, residual, o_weight, gain, routes, gates, w_gate, w_up, w_down):
    head_replicas = QUERY_HEADS // KEY_VALUE_HEADS
    selector_index = jnp.arange(QUERY_HEADS, dtype=jnp.int32) // head_replicas
    q_heads = query.reshape(PROMPT_TOKENS, QUERY_HEADS, HEAD_DIMENSION).transpose(1, 0, 2)
    key_head_tensor = keys.reshape(PROMPT_TOKENS, KEY_VALUE_HEADS, HEAD_DIMENSION).transpose(1, 0, 2)[selector_index]
    value_head_tensor = values.reshape(PROMPT_TOKENS, KEY_VALUE_HEADS, HEAD_DIMENSION).transpose(1, 0, 2)[selector_index]
    attended = lax.map(attend_one, (q_heads, key_head_tensor, value_head_tensor))
    attended = attended.transpose(1, 0, 2).reshape(PROMPT_TOKENS, QUERY_HEADS * HEAD_DIMENSION)
    projected = jnp.dot(attended, o_weight, preferred_element_type=jnp.float32)
    mixed = (projected + residual.astype(jnp.float32)).astype(jnp.bfloat16)
    mixed_f = mixed.astype(jnp.float32)
    normed = (mixed_f * lax.rsqrt(lax.optimization_barrier(jnp.mean(mixed_f * mixed_f, axis=-1, keepdims=True)) + 1e-06) * gain).astype(jnp.bfloat16)
    sources = N_CTX * N_HEAD
    expert_ids = routes.reshape(sources, TOK_OWN * TOPK)
    onehot = (expert_ids[..., None] == jnp.arange(EXPERTS, dtype=jnp.int32)).astype(jnp.int32)
    slots = lax.optimization_barrier(jnp.sum((jnp.cumsum(onehot, axis=1) - 1) * onehot, axis=-1)).astype(jnp.int32)
    token_ids = (jnp.arange(PROMPT_TOKENS * TOPK, dtype=jnp.int32) // TOPK).reshape(sources, TOK_OWN * TOPK)
    source_ids = jnp.arange(sources, dtype=jnp.int32)[:, None]
    columns = (source_ids * CAP + slots).astype(jnp.int32)
    weight_norm = gates / lax.optimization_barrier(jnp.sum(gates, axis=-1, keepdims=True))
    table = jnp.full((EXPERTS, sources * CAP), PROMPT_TOKENS, dtype=jnp.int32).at[expert_ids, columns].set(token_ids)
    weight_table = jnp.zeros((EXPERTS, sources * CAP), jnp.float32).at[expert_ids, columns].set(weight_norm.reshape(sources, -1))
    padded = jnp.concatenate([normed, jnp.zeros((1, D), jnp.bfloat16)], axis=0)

    def expert_step(running, operands):
        row_ids, row_weights, gate_proj, up_proj, down_proj = operands
        inputs = padded[row_ids]
        gate_act = jnp.dot(inputs, gate_proj, preferred_element_type=jnp.float32)
        up_act = jnp.dot(inputs, up_proj, preferred_element_type=jnp.float32)
        hidden = (jax.nn.silu(gate_act) * up_act).astype(jnp.bfloat16)
        output = jnp.dot(hidden, down_proj, preferred_element_type=jnp.float32).astype(jnp.bfloat16)
        return (running.at[row_ids].add(output.astype(jnp.float32) * row_weights[:, None]), None)
    running, _ = lax.scan(expert_step, jnp.zeros((PROMPT_TOKENS + 1, D), jnp.float32), (table, weight_table, w_gate, w_up, w_down))
    expert_mix = running[:PROMPT_TOKENS].astype(jnp.bfloat16)
    return (mixed, expert_mix)
```

```python
import functools

import jax
import jax.numpy as jnp
from jax import lax
from jax.experimental import pallas as pl
from jax.experimental.pallas import tpu as pltpu
from jax.sharding import PartitionSpec as P

HEAD_DIMENSION = 128
CHUNKS = ((0, 1, 2, 3),)


def expert_apply(arrived, gate_proj, up_proj, down_proj):
    shape_in = arrived.shape
    flat_rows = arrived.reshape(-1, shape_in[-1])
    gate_act = jnp.dot(flat_rows, gate_proj, preferred_element_type=jnp.float32)
    up_act = jnp.dot(flat_rows, up_proj, preferred_element_type=jnp.float32)
    hidden = (jax.nn.silu(gate_act) * up_act).astype(jnp.bfloat16)
    output = jnp.dot(hidden, down_proj, preferred_element_type=jnp.float32).astype(jnp.bfloat16)
    return output.reshape(shape_in)


def sparse_body(query, keys, values, residual, o_weight, gain, routes, gates, w_gate, w_up, w_down):
    head_size = HEAD_DIMENSION
    query_rows = query.shape[0]
    kv_heads = keys.shape[1] // head_size
    q_heads = query.shape[1] // head_size
    head_replicas = q_heads // kv_heads
    scale = head_size ** (-0.5)
    queries = query.reshape(query_rows, kv_heads, head_replicas, head_size)
    first_pos = lax.axis_index("ctx") * query_rows
    query_pos = first_pos + jnp.arange(query_rows, dtype=jnp.int32)
    key_all = lax.all_gather(keys, "ctx", axis=0, tiled=True)
    value_all = lax.all_gather(values, "ctx", axis=0, tiled=True)
    width = key_all.shape[0]
    visible = jnp.arange(width, dtype=jnp.int32)[None, :] <= query_pos[:, None]
    scores = (
        jnp.einsum(
            "veqi,zei->eqvz",
            queries,
            key_all.reshape(width, kv_heads, head_size),
            preferred_element_type=jnp.float32,
        )
        * scale
    )
    scores = jnp.where(visible, scores, -1e30)
    top = jnp.max(scores, axis=-1)
    weights = jnp.where(visible, jnp.exp(scores - top[..., None]), 0.0)
    total = jnp.sum(weights, axis=-1)
    summed_values = jnp.einsum(
        "pexa,apo->pexo",
        weights.astype(jnp.bfloat16),
        value_all.reshape(width, kv_heads, head_size),
        preferred_element_type=jnp.float32,
    )
    attended = (
        (summed_values / total[..., None])
        .transpose(2, 0, 1, 3)
        .reshape(query_rows, q_heads * head_size)
        .astype(jnp.bfloat16)
    )
    head_terms = jnp.dot(
        attended,
        lax.all_gather(o_weight, "ctx", axis=1, tiled=True),
        preferred_element_type=jnp.float32,
    )
    summed = lax.psum_scatter(
        head_terms.astype(jnp.bfloat16), "head", scatter_dimension=0, tiled=True
    ).astype(jnp.float32)
    mixed = (summed + residual.astype(jnp.float32)).astype(jnp.bfloat16)
    mixed_f = mixed.astype(jnp.float32)
    normed = (
        mixed_f * lax.rsqrt(jnp.mean(mixed_f * mixed_f, axis=-1, keepdims=True) + 1e-06) * gain
    ).astype(jnp.bfloat16)
    own_rows = residual.shape[0]
    model_dim = residual.shape[1]
    top_count = routes.shape[1]
    devices = lax.axis_size("ctx") * lax.axis_size("head")
    capacity = slots_per_expert(own_rows, top_count, devices)
    expert_ids = routes.reshape(-1)
    onehot = (expert_ids[:, None] == jnp.arange(devices, dtype=jnp.int32)[None, :]).astype(
        jnp.int32
    )
    slots = jnp.sum((jnp.cumsum(onehot, axis=0) - 1) * onehot, axis=1)
    target = expert_ids * capacity + slots
    outgoing = (
        jnp.zeros((devices * capacity, model_dim), jnp.bfloat16)
        .at[target]
        .set(jnp.repeat(normed, top_count, axis=0))
    )
    outgoing = outgoing.reshape(devices, capacity, model_dim)
    computed = expert_apply(
        lax.all_to_all(outgoing, ("ctx", "head"), split_axis=0, concat_axis=0, tiled=True),
        w_gate[0],
        w_up[0],
        w_down[0],
    )
    returned = lax.all_to_all(computed, ("ctx", "head"), split_axis=0, concat_axis=0, tiled=True)
    selected_entries = returned.reshape(devices * capacity, model_dim)[target]
    selected_entries = selected_entries.astype(jnp.float32).reshape(own_rows, top_count, model_dim)
    weight_norm = gates / jnp.sum(gates, axis=-1, keepdims=True)
    expert_mix = jnp.sum(selected_entries * weight_norm[..., None], axis=1).astype(jnp.bfloat16)
    return (mixed, expert_mix)


def slots_per_expert(own_rows, top_count, devices):
    return min(own_rows, max(2, 2 * own_rows * top_count // devices))


def place():
    return lax.axis_index("ctx"), lax.axis_index("head")


def shift(x, by):
    n = lax.axis_size("ctx")
    return lax.ppermute(x, "ctx", [(i, (i + by) % n) for i in range(n)])


def swap(x, mask):
    n = lax.axis_size("head")
    return lax.ppermute(x, "head", [(i, i ^ mask) for i in range(n)])


def attend_kernel(steps, n_ctx, n_head, *refs):
    n = len(steps)
    q_refs, kv_refs, w_ref = refs[:n], refs[n : n + n_ctx], refs[n + n_ctx]
    own_ref = refs[n + n_ctx + 1]
    send_refs = refs[n + n_ctx + 2 : n + n_ctx + 1 + n_head]
    k_all, v_all, att, prod = refs[n + n_ctx + 1 + n_head :]
    hd = HEAD_DIMENSION
    rows = q_refs[0].shape[0]
    width = kv_refs[0].shape[0]
    own_rows = rows // n_head
    c, h = place()
    key_pos = []
    for m in range(n_ctx):
        k_all[m * width : (m + 1) * width, :] = kv_refs[m][:, :hd]
        v_all[m * width : (m + 1) * width, :] = kv_refs[m][:, hd:]
        block = lax.rem(c - m + n_ctx, n_ctx)
        key_pos.append(block * width + lax.broadcasted_iota(jnp.int32, (rows, width), 1))
    key_pos = jnp.concatenate(key_pos, axis=1)
    row_pos = lax.broadcasted_iota(jnp.int32, (rows, 1), 0)
    scale = hd**-0.5
    for i, step in enumerate(steps):
        first = lax.rem(c - step + n_ctx, n_ctx) * rows
        visible = key_pos <= first + row_pos
        for g in range(q_refs[i].shape[1] // hd):
            cols = slice(g * hd, (g + 1) * hd)
            scores = lax.dot_general(
                q_refs[i][:, cols],
                k_all[...],
                (((1,), (1,)), ((), ())),
                preferred_element_type=jnp.float32,
            )
            scores = jnp.where(visible, scores, -1e30)
            top = jnp.max(scores, axis=-1, keepdims=True)
            weights = jnp.exp((scores - top) * scale)
            total = jnp.sum(weights, axis=-1, keepdims=True)
            summed = jnp.dot(
                weights.astype(jnp.bfloat16), v_all[...], preferred_element_type=jnp.float32
            )
            att[:, cols] = (summed / total).astype(jnp.bfloat16)
        prod[...] = jnp.dot(att[...], w_ref[...], preferred_element_type=jnp.float32)
        own_ref[i] = prod[pl.ds(pl.multiple_of(h * own_rows, own_rows), own_rows), :]
        for j in range(1, n_head):
            other = jnp.bitwise_xor(h, j)
            start = pl.multiple_of(other * own_rows, own_rows)
            send_refs[j - 1][i] = prod[pl.ds(start, own_rows), :].astype(jnp.bfloat16)


def attend(steps, q_list, kv_list, o_weight):
    n_ctx, n_head = lax.axis_size("ctx"), lax.axis_size("head")
    rows, q_cols = q_list[0].shape
    width = kv_list[0].shape[0]
    out_cols = o_weight.shape[1]
    n = len(steps)
    piece = (n, rows // n_head, out_cols)
    vmem = pl.BlockSpec(memory_space=pltpu.VMEM)
    flops = 4 * n * rows * q_cols * width * n_ctx + 2 * n * rows * q_cols * out_cols
    return pl.pallas_call(
        functools.partial(attend_kernel, steps, n_ctx, n_head),
        out_shape=[jax.ShapeDtypeStruct(piece, jnp.float32)]
        + [jax.ShapeDtypeStruct(piece, jnp.bfloat16)] * (n_head - 1),
        in_specs=[vmem] * (n + n_ctx + 1),
        out_specs=[vmem] * n_head,
        scratch_shapes=[
            pltpu.VMEM((width * n_ctx, HEAD_DIMENSION), jnp.bfloat16),
            pltpu.VMEM((width * n_ctx, HEAD_DIMENSION), jnp.bfloat16),
            pltpu.VMEM((rows, q_cols), jnp.bfloat16),
            pltpu.VMEM((rows, out_cols), jnp.float32),
        ],
        cost_estimate=pl.CostEstimate(
            flops=flops, bytes_accessed=2 * q_cols * out_cols, transcendentals=flops // 512
        ),
        name="attend",
    )(*q_list, *kv_list, o_weight)


def expert_kernel(chunks, n_ctx, n_head, *refs):
    n_pieces = len(chunks) * n_head * n_ctx
    pieces, refs = refs[:n_pieces], refs[n_pieces:]
    share_refs, refs = refs[:n_head], refs[n_head:]
    gain_ref, gate_ref, up_ref, down_ref = refs[:4]
    keep_ref, send_ref, mixed_ref = refs[4:7]
    x_ref, acc_ref, share_ref = refs[7:]
    step = pl.program_id(0)
    own_rows = mixed_ref.shape[0]
    cols = pieces[0].shape[-1]
    c, h = place()

    def row_block(j, t):
        return (((j % 2) * (n_head // 2) + j // 2) * n_ctx + t) * own_rows

    @pl.when(step == 0)
    def _():
        expert = c * n_head + h
        for j in range(n_head):
            lanes = lax.broadcasted_iota(jnp.int32, share_refs[j].shape[1:], 1)
            for t in range(n_ctx):
                start = row_block(j, t)
                shares = jnp.where(lanes == expert, share_refs[j][t], 0.0)
                share_ref[start : start + own_rows, :] = jnp.sum(shares, axis=-1, keepdims=True)
        for j in range(n_head):
            for t in range(n_ctx):
                start = row_block(j, t)
                blocks = []
                square = jnp.zeros((own_rows, 1), jnp.float32)
                for m in range(n_ctx):
                    s = (t - m) % n_ctx
                    for k, steps in enumerate(chunks):
                        if s in steps:
                            ref = pieces[(k * n_head + j) * n_ctx + m]
                            block = ref[steps.index(s)]
                    block_f = block.astype(jnp.float32)
                    square += jnp.sum(block_f * block_f, axis=-1, keepdims=True)
                    col = lax.rem(c - m + n_ctx, n_ctx)
                    blocks.append((block_f, col))
                    if j == 0 and t == 0:
                        mixed_ref[:, pl.ds(pl.multiple_of(col * cols, cols), cols)] = block
                root = lax.rsqrt(square / (cols * n_ctx) + 1e-06)
                for block_f, col in blocks:
                    at = pl.ds(pl.multiple_of(col * cols, cols), cols)
                    x_ref[start : start + own_rows, at] = (
                        block_f * root * gain_ref[:, at]
                    ).astype(jnp.bfloat16)

    gate = jnp.dot(x_ref[...], gate_ref[0], preferred_element_type=jnp.float32)
    up = jnp.dot(x_ref[...], up_ref[0], preferred_element_type=jnp.float32)
    hidden = (gate * jax.nn.sigmoid(gate) * up).astype(jnp.bfloat16)
    out = jnp.dot(hidden, down_ref[0], preferred_element_type=jnp.float32)

    @pl.when(step == 0)
    def _():
        acc_ref[...] = out

    @pl.when((step > 0) & (step < pl.num_programs(0) - 1))
    def _():
        acc_ref[...] += out

    @pl.when(step == pl.num_programs(0) - 1)
    def _():
        final = ((acc_ref[...] + out) * share_ref[...]).astype(jnp.bfloat16)
        half = final.shape[0] // 2
        keep_ref[...] = final[:half].reshape(keep_ref.shape)
        send_ref[...] = final[half:].reshape(send_ref.shape)


def experts(chunks, pieces, shares, gain, w_gate, w_up, w_down, own_rows):
    n_ctx, n_head = lax.axis_size("ctx"), lax.axis_size("head")
    dim, hidden = w_gate.shape[1:]
    rows = own_rows * n_ctx * n_head
    tile = hidden // 3
    vmem = pl.BlockSpec(memory_space=pltpu.VMEM)
    out_half = jax.ShapeDtypeStruct((n_head // 2, n_ctx, own_rows, dim), jnp.bfloat16)
    return pl.pallas_call(
        functools.partial(expert_kernel, chunks, n_ctx, n_head),
        grid=(hidden // tile,),
        out_shape=[out_half, out_half, jax.ShapeDtypeStruct((own_rows, dim), jnp.bfloat16)],
        in_specs=[vmem] * (len(pieces) + len(shares) + 1)
        + [
            pl.BlockSpec((1, dim, tile), lambda f: (0, 0, f)),
            pl.BlockSpec((1, dim, tile), lambda f: (0, 0, f)),
            pl.BlockSpec((1, tile, dim), lambda f: (0, f, 0)),
        ],
        out_specs=[vmem] * 3,
        scratch_shapes=[
            pltpu.VMEM((rows, dim), jnp.bfloat16),
            pltpu.VMEM((rows, dim), jnp.float32),
            pltpu.VMEM((rows, 1), jnp.float32),
        ],
        cost_estimate=pl.CostEstimate(
            flops=6 * rows * dim * hidden, bytes_accessed=6 * dim * hidden, transcendentals=0
        ),
        name="experts",
    )(*pieces, *shares, gain.reshape(1, -1), w_gate, w_up, w_down)


def dense_body(query, keys, values, residual, o_weight, gain, routes, gates, w_gate, w_up, w_down):
    n_ctx, n_head = lax.axis_size("ctx"), lax.axis_size("head")
    own_rows, dim = residual.shape
    cols = o_weight.shape[1]
    c, h = place()

    kv_list = [jnp.concatenate([keys, values], axis=1)]
    q_list = [query]
    for _ in range(n_ctx - 1):
        kv_list.append(shift(kv_list[-1], 1))
        q_list.append(shift(q_list[-1], 1))

    share = gates / jnp.sum(gates, axis=-1, keepdims=True)
    ids = jnp.arange(n_ctx * n_head, dtype=jnp.int32)
    table = jnp.sum(jnp.where(routes[..., None] == ids, share[..., None], 0.0), axis=1)
    table = jnp.stack([table] + [shift(table, t) for t in range(1, n_ctx)])
    shares = [table]
    bit = n_head // 2
    while bit:
        shares = shares + [swap(s, bit) for s in shares]
        bit //= 2
    order = head_order(n_head)
    shares = [shares[order.index(j)] for j in range(n_head)]

    by_tile = residual.reshape(own_rows, n_ctx, cols)
    skip = []
    for s in range(n_ctx):
        part = lax.dynamic_index_in_dim(by_tile, lax.rem(c + s, n_ctx), axis=1, keepdims=False)
        skip.append(shift(part, s) if s else part)

    pieces = []
    for steps in CHUNKS:
        own, *sends = attend(steps, [q_list[s] for s in steps], kv_list, o_weight)
        total = own
        for j, send in enumerate(sends, 1):
            total = total + swap(send, j).astype(jnp.float32)
        total = total + jnp.stack([skip[s] for s in steps]).astype(jnp.float32)
        piece = total.astype(jnp.bfloat16)
        got = [[piece] + [shift(piece, m) for m in range(1, n_ctx)]]
        bit = n_head // 2
        while bit:
            got = got + [[swap(x, bit) for x in row] for row in got]
            bit //= 2
        pieces += [x for j in range(n_head) for x in got[order.index(j)]]

    keep, send, mixed = experts(CHUNKS, pieces, shares, gain, w_gate, w_up, w_down, own_rows)

    both = keep.astype(jnp.float32) + swap(send, 1).astype(jnp.float32)
    across = swap(both[1].astype(jnp.bfloat16), 2)
    column = (both[0] + across.astype(jnp.float32)).astype(jnp.bfloat16)
    result = column[0].astype(jnp.float32)
    for t in range(1, n_ctx):
        result = result + shift(column[t], -t).astype(jnp.float32)
    return (mixed, result.astype(jnp.bfloat16))


def head_order(n_head):
    order = [0]
    bit = n_head // 2
    while bit:
        order = order + [j ^ bit for j in order]
        bit //= 2
    return order


def body(*args):
    residual, routes = args[3], args[6]
    own_rows, dim = residual.shape
    n_ctx, n_head = lax.axis_size("ctx"), lax.axis_size("head")
    dense = slots_per_expert(own_rows, routes.shape[1], n_ctx * n_head) == own_rows
    dense = dense and n_ctx == 4 and n_head == 4 and (dim // n_ctx) % 128 == 0
    return (dense_body if dense else sparse_body)(*args)


def solution(mesh):
    return jax.shard_map(
        body,
        mesh=mesh,
        in_specs=(
            P(("group", "ctx"), "head"),
            P(("group", "ctx"), "head"),
            P(("group", "ctx"), "head"),
            P(("group", "ctx", "head"), None),
            P("head", "ctx"),
            P(),
            P(("group", "ctx", "head"), None),
            P(("group", "ctx", "head"), None),
            P(("ctx", "head"), None, None),
            P(("ctx", "head"), None, None),
            P(("ctx", "head"), None, None),
        ),
        out_specs=(P(("group", "ctx", "head"), None), P(("group", "ctx", "head"), None)),
        check_vma=False,
    )
```

```python
import functools

import jax
import jax.numpy as jnp
from jax import lax
from jax.experimental import pallas as pl
from jax.experimental.pallas import tpu as pltpu
from jax.sharding import PartitionSpec as P


HEAD_DIMENSION = 128
LANES = 64


def expert_apply(arrived, gate_proj, up_proj, down_proj):
    shape_in = arrived.shape
    flat_rows = arrived.reshape(-1, shape_in[-1])
    gate_act = jnp.dot(flat_rows, gate_proj, preferred_element_type=jnp.float32)
    up_act = jnp.dot(flat_rows, up_proj, preferred_element_type=jnp.float32)
    hidden = (jax.nn.silu(gate_act) * up_act).astype(jnp.bfloat16)
    output = jnp.dot(hidden, down_proj, preferred_element_type=jnp.float32).astype(jnp.bfloat16)
    return output.reshape(shape_in)


def sparse_body(query, keys, values, residual, o_weight, gain, routes, gates, w_gate, w_up, w_down):
    head_size = HEAD_DIMENSION
    query_rows = query.shape[0]
    kv_heads = keys.shape[1] // head_size
    q_heads = query.shape[1] // head_size
    head_replicas = q_heads // kv_heads
    scale = head_size ** (-0.5)
    queries = query.reshape(query_rows, kv_heads, head_replicas, head_size)
    first_pos = lax.axis_index("ctx") * query_rows
    query_pos = first_pos + jnp.arange(query_rows, dtype=jnp.int32)
    key_all = lax.all_gather(keys, "ctx", axis=0, tiled=True)
    value_all = lax.all_gather(values, "ctx", axis=0, tiled=True)
    width = key_all.shape[0]
    visible = jnp.arange(width, dtype=jnp.int32)[None, :] <= query_pos[:, None]
    scores = (
        jnp.einsum(
            "veqi,zei->eqvz",
            queries,
            key_all.reshape(width, kv_heads, head_size),
            preferred_element_type=jnp.float32,
        )
        * scale
    )
    scores = jnp.where(visible, scores, -1e30)
    top = jnp.max(scores, axis=-1)
    weights = jnp.where(visible, jnp.exp(scores - top[..., None]), 0.0)
    total = jnp.sum(weights, axis=-1)
    summed_values = jnp.einsum(
        "pexa,apo->pexo",
        weights.astype(jnp.bfloat16),
        value_all.reshape(width, kv_heads, head_size),
        preferred_element_type=jnp.float32,
    )
    attended = (
        (summed_values / total[..., None])
        .transpose(2, 0, 1, 3)
        .reshape(query_rows, q_heads * head_size)
        .astype(jnp.bfloat16)
    )
    head_terms = jnp.dot(
        attended,
        lax.all_gather(o_weight, "ctx", axis=1, tiled=True),
        preferred_element_type=jnp.float32,
    )
    summed = lax.psum_scatter(
        head_terms.astype(jnp.bfloat16), "head", scatter_dimension=0, tiled=True
    ).astype(jnp.float32)
    mixed = (summed + residual.astype(jnp.float32)).astype(jnp.bfloat16)
    mixed_f = mixed.astype(jnp.float32)
    normed = (
        mixed_f * lax.rsqrt(jnp.mean(mixed_f * mixed_f, axis=-1, keepdims=True) + 1e-06) * gain
    ).astype(jnp.bfloat16)
    own_rows = residual.shape[0]
    model_dim = residual.shape[1]
    top_count = routes.shape[1]
    devices = lax.axis_size("ctx") * lax.axis_size("head")
    capacity = slots_per_expert(own_rows, top_count, devices)
    expert_ids = routes.reshape(-1)
    onehot = (expert_ids[:, None] == jnp.arange(devices, dtype=jnp.int32)[None, :]).astype(
        jnp.int32
    )
    slots = jnp.sum((jnp.cumsum(onehot, axis=0) - 1) * onehot, axis=1)
    target = expert_ids * capacity + slots
    outgoing = (
        jnp.zeros((devices * capacity, model_dim), jnp.bfloat16)
        .at[target]
        .set(jnp.repeat(normed, top_count, axis=0))
    )
    outgoing = outgoing.reshape(devices, capacity, model_dim)
    computed = expert_apply(
        lax.all_to_all(outgoing, ("ctx", "head"), split_axis=0, concat_axis=0, tiled=True),
        w_gate[0],
        w_up[0],
        w_down[0],
    )
    returned = lax.all_to_all(computed, ("ctx", "head"), split_axis=0, concat_axis=0, tiled=True)
    selected_entries = returned.reshape(devices * capacity, model_dim)[target]
    selected_entries = selected_entries.astype(jnp.float32).reshape(own_rows, top_count, model_dim)
    weight_norm = gates / jnp.sum(gates, axis=-1, keepdims=True)
    expert_mix = jnp.sum(selected_entries * weight_norm[..., None], axis=1).astype(jnp.bfloat16)
    return (mixed, expert_mix)


def slots_per_expert(own_rows, top_count, devices):
    return min(own_rows, max(2, 2 * own_rows * top_count // devices))


def place():
    return lax.axis_index("ctx"), lax.axis_index("head")


def ring_at(position):
    return position ^ (position >> 1)


def behind(steps):
    n = lax.axis_size("ctx")
    c = lax.axis_index("ctx")
    return ring_at(jnp.bitwise_and(ring_at(c) - steps + n, n - 1))


def shift(x, by):
    n = lax.axis_size("ctx")
    pairs = [(ring_at(i), ring_at((i + by) % n)) for i in range(n)]
    return lax.ppermute(x, "ctx", pairs)


def swap(x, mask):
    n = lax.axis_size("head")
    return lax.ppermute(x, "head", [(i, i ^ mask) for i in range(n)])


def call(kernel, args, out_shape, scratch, flops, moved, limit):
    vmem = pl.BlockSpec(memory_space=pltpu.VMEM)
    return pl.pallas_call(
        kernel,
        out_shape=out_shape,
        in_specs=[vmem] * len(args),
        out_specs=[vmem] * len(out_shape),
        scratch_shapes=scratch,
        cost_estimate=pl.CostEstimate(flops=flops, bytes_accessed=moved, transcendentals=0),
        compiler_params=pltpu.CompilerParams(vmem_limit_bytes=limit << 20),
    )(*args)


def prepare_kernel(n_ctx, k_ref, v_ref, skip_ref, route_ref, gate_ref, *out_refs):
    hd = HEAD_DIMENSION
    gates = gate_ref[...].T
    routes = route_ref[...].T
    share = gates / jnp.sum(gates, axis=-1, keepdims=True)
    own_rows, dim = skip_ref.shape
    lanes = lax.broadcasted_iota(jnp.int32, (own_rows, 2 * LANES), 1)
    table = jnp.zeros((own_rows, 2 * LANES), jnp.float32)
    for k in range(gates.shape[1]):
        table += jnp.where(lanes % LANES == routes[:, k : k + 1], share[:, k : k + 1], 0.0)
    high = table.astype(jnp.bfloat16).astype(jnp.float32)
    packed = jnp.where(lanes < LANES, high, table - high).astype(jnp.bfloat16)
    rows = k_ref.shape[0]
    width = 2 * hd
    for s, out_ref in enumerate(out_refs):
        out_ref[:rows, :hd] = k_ref[...]
        out_ref[:rows, hd:] = v_ref[...]
        first = behind(-s) * (dim // n_ctx)
        at = rows
        for i in range(dim // n_ctx // width):
            cols = pl.ds(pl.multiple_of(first + i * width, width), width)
            out_ref[at : at + own_rows, :] = skip_ref[:, cols]
            at += own_rows
        out_ref[at:, : 2 * LANES] = packed
        out_ref[at:, 2 * LANES :] = jnp.zeros((own_rows, width - 2 * LANES), jnp.bfloat16)


def prepare(keys, values, residual, routes, gates):
    n_ctx = lax.axis_size("ctx")
    own_rows, dim = residual.shape
    rows = keys.shape[0] + own_rows * (dim // n_ctx // (2 * HEAD_DIMENSION) + 1)
    part = jax.ShapeDtypeStruct((rows, 2 * HEAD_DIMENSION), jnp.bfloat16)
    args = (keys, values, residual, routes.T, gates.T)
    kernel = functools.partial(prepare_kernel, n_ctx)
    return call(kernel, args, [part] * n_ctx, [], 0, 1 << 18, 4)


def attend_kernel(steps, n_before, n_ctx, n_head, *refs):
    n = len(steps)
    q_refs, refs = refs[:n], refs[n:]
    part_refs, refs = refs[:n_ctx], refs[n_ctx:]
    w_ref, refs = refs[0], refs[1:]
    if n_before:
        before, refs = refs[:n_head], refs[n_head:]
    out_refs, (k_all, v_all, queries, att, prod) = refs[:n_head], refs[n_head:]
    hd = HEAD_DIMENSION
    rows, q_cols = q_refs[0].shape
    own_rows = rows // n_head
    heads = q_cols // hd
    together = 4
    _, h = place()
    key_pos = []
    for m in range(n_ctx):
        k_all[m * rows : (m + 1) * rows, :] = part_refs[m][:rows, :hd]
        v_all[m * rows : (m + 1) * rows, :] = part_refs[m][:rows, hd:]
        key_pos.append(behind(m) * rows + lax.broadcasted_iota(jnp.int32, (rows, rows), 1))
    key_pos = jnp.concatenate(key_pos, axis=1)
    row_pos = lax.broadcasted_iota(jnp.int32, (rows, 1), 0)
    scale = hd**-0.5
    for j in range(n_head if n_before else 0):
        out_refs[j][:n_before] = before[j][...]
    for i, step in enumerate(steps):
        visible = key_pos <= behind(step) * rows + row_pos
        for g in range(heads):
            queries[g * rows : (g + 1) * rows, :] = q_refs[i][:, g * hd : (g + 1) * hd]
        for g in range(0, heads, together):
            scores = lax.dot_general(
                queries[g * rows : (g + together) * rows, :],
                k_all[...],
                (((1,), (1,)), ((), ())),
                preferred_element_type=jnp.float32,
            ).reshape(together, rows, -1)
            scores = jnp.where(visible[None], scores, -1e30)
            top = jnp.max(scores, axis=-1, keepdims=True)
            weights = jnp.exp((scores - top) * scale)
            total = jnp.sum(weights, axis=-1, keepdims=True)
            summed = jnp.dot(
                weights.astype(jnp.bfloat16).reshape(together * rows, -1),
                v_all[...],
                preferred_element_type=jnp.float32,
            ).reshape(together, rows, hd)
            done = (summed * (1.0 / total)).astype(jnp.bfloat16)
            for k in range(together):
                att[:, (g + k) * hd : (g + k + 1) * hd] = done[k]
        prod[...] = jnp.dot(att[...], w_ref[...], preferred_element_type=jnp.float32)
        for j in range(n_head):
            start = pl.multiple_of(jnp.bitwise_xor(h, j) * own_rows, own_rows)
            block = prod[pl.ds(start, own_rows), :]
            out_refs[j][n_before + i] = block.astype(out_refs[j].dtype)


def attend(steps, q_list, parts, o_weight, before):
    n_ctx, n_head = lax.axis_size("ctx"), lax.axis_size("head")
    rows, q_cols = q_list[0].shape
    out_cols = o_weight.shape[1]
    n = len(steps)
    n_before = before[0].shape[0] if before else 0
    piece = (n_before + n, rows // n_head, out_cols)
    out_shape = [jax.ShapeDtypeStruct(piece, jnp.float32)]
    out_shape += [jax.ShapeDtypeStruct(piece, jnp.bfloat16)] * (n_head - 1)
    kernel = functools.partial(attend_kernel, steps, n_before, n_ctx, n_head)
    scratch = [
        pltpu.VMEM((rows * n_ctx, HEAD_DIMENSION), jnp.bfloat16),
        pltpu.VMEM((rows * n_ctx, HEAD_DIMENSION), jnp.bfloat16),
        pltpu.VMEM((rows * q_cols // HEAD_DIMENSION, HEAD_DIMENSION), jnp.bfloat16),
        pltpu.VMEM((rows, q_cols), jnp.bfloat16),
        pltpu.VMEM((rows, out_cols), jnp.float32),
    ]
    flops = n * (4 * rows * q_cols * rows * n_ctx + 2 * rows * q_cols * out_cols)
    args = (*q_list, *parts, o_weight, *before)
    return call(kernel, args, out_shape, scratch, flops, 2 * q_cols * out_cols, 16)


def combine_kernel(n_ctx, sizes, n_head, *refs):
    sums, refs = refs[: n_head * len(sizes)], refs[n_head * len(sizes) :]
    part_refs, (piece_ref, shared_ref) = refs[:n_ctx], refs[n_ctx:]
    own_rows, cols = piece_ref.shape[1:]
    width = part_refs[0].shape[1]
    base = part_refs[0].shape[0] - own_rows * (cols // width + 1)
    s = 0
    for k, size in enumerate(sizes):
        for i in range(size):
            total = sums[k * n_head][i]
            for j in range(1, n_head):
                total += sums[k * n_head + j][i].astype(jnp.float32)
            for b in range(cols // width):
                at = slice(b * width, (b + 1) * width)
                first = base + b * own_rows
                skip = part_refs[s][first : first + own_rows, :].astype(jnp.float32)
                block = (total[:, at] + skip).astype(jnp.bfloat16)
                piece_ref[s, :, at] = block
                shared_ref[s, :, at] = block
            shared_ref[s, :, cols:] = part_refs[s][base + cols // width * own_rows :, : 2 * LANES]
            s += 1


def combine(sums, parts, sizes):
    n_ctx, n_head = lax.axis_size("ctx"), lax.axis_size("head")
    _, own_rows, cols = sums[0].shape
    out_shape = [
        jax.ShapeDtypeStruct((n_ctx, own_rows, cols), jnp.bfloat16),
        jax.ShapeDtypeStruct((n_ctx, own_rows, cols + 2 * LANES), jnp.bfloat16),
    ]
    kernel = functools.partial(combine_kernel, n_ctx, sizes, n_head)
    return call(kernel, (*sums, *parts), out_shape, [], 0, 1 << 20, 4)


def expert_kernel(n_ctx, halves, *refs):
    pieces, refs = refs[:n_ctx], refs[n_ctx:]
    gain_ref, refs = refs[0], refs[1:]
    weights, refs = (refs[:3], refs[3:6]), refs[6:]
    outs, (x_ref, acc_ref, share_ref) = refs[:-3], refs[-3:]
    own_rows, cols = pieces[1].shape[1:]
    c, h = place()

    for t in range(n_ctx):
        blocks = []
        square = jnp.zeros((own_rows, 1), jnp.float32)
        for m in range(n_ctx):
            block = pieces[m][(t - m) % n_ctx, :, :cols]
            block_f = block.astype(jnp.float32)
            square += jnp.sum(block_f * block_f, axis=-1, keepdims=True)
            at = pl.ds(pl.multiple_of(behind(m) * cols, cols), cols)
            blocks.append((block_f, at))
            if halves is None and t == 0:
                outs[1][:, at] = block
        root = lax.rsqrt(square / (cols * n_ctx) + 1e-06)
        here = slice(t * own_rows, (t + 1) * own_rows)
        for block_f, at in blocks:
            x_ref[here, at] = (block_f * root * gain_ref[:, at]).astype(jnp.bfloat16)
        share_ref[here, :] = pieces[0][t, :, cols:].astype(jnp.float32)

    lanes = lax.broadcasted_iota(jnp.int32, share_ref.shape, 1) % LANES
    for i, (gate_ref, up_ref, down_ref) in enumerate(weights):
        expert = c * lax.axis_size("head") + jnp.bitwise_xor(h, i)
        share = jnp.sum(jnp.where(lanes == expert, share_ref[...], 0.0), axis=-1, keepdims=True)
        gate = jnp.dot(x_ref[...], gate_ref[0], preferred_element_type=jnp.float32)
        up = jnp.dot(x_ref[...], up_ref[0], preferred_element_type=jnp.float32)
        hidden = (gate * jax.nn.sigmoid(gate) * up).astype(jnp.bfloat16)
        out = jnp.dot(hidden, down_ref[0], preferred_element_type=jnp.float32) * share
        if i == 0:
            acc_ref[...] = out
        elif halves is None:
            outs[0][...] = (acc_ref[...] + out).reshape(outs[0].shape)
        else:
            total = (acc_ref[...] + out).astype(jnp.bfloat16)
            for out_ref, half in zip(outs, halves):
                for at, t in enumerate(half):
                    out_ref[at] = total[t * own_rows : (t + 1) * own_rows, :]


def experts(pieces, gain, weights, halves):
    n_ctx, own_rows, _ = pieces[0].shape
    _, dim, hidden = weights[0].shape
    rows = own_rows * n_ctx
    if halves is None:
        out_shape = [
            jax.ShapeDtypeStruct((n_ctx, own_rows, dim), jnp.float32),
            jax.ShapeDtypeStruct((own_rows, dim), jnp.bfloat16),
        ]
    else:
        out_shape = [
            jax.ShapeDtypeStruct((len(half), own_rows, dim), jnp.bfloat16) for half in halves
        ]
    scratch = [
        pltpu.VMEM((rows, dim), jnp.bfloat16),
        pltpu.VMEM((rows, dim), jnp.float32),
        pltpu.VMEM((rows, 2 * LANES), jnp.float32),
    ]
    args = (*pieces, gain.reshape(1, -1), *weights)
    kernel = functools.partial(expert_kernel, n_ctx, halves)
    flops = 12 * rows * dim * hidden
    return call(kernel, args, out_shape, scratch, flops, 12 * dim * hidden, 28)


def dense_body(query, keys, values, residual, o_weight, gain, routes, gates, w_gate, w_up, w_down):
    q_list = [query]
    for _ in range(3):
        q_list.append(shift(q_list[-1], 1))
    parts = prepare(keys, values, residual, routes, gates)
    parts = [parts[0]] + [shift(parts[s], s) for s in (1, 2, 3)]

    weights = [w_gate, w_up, w_down]
    weights += [swap(w, 1) for w in weights]

    first = attend((0, 1), q_list[:2], parts, o_weight, ())
    later = attend((2,), q_list[2:3], parts, o_weight, ())
    later = attend((3,), q_list[3:], parts, o_weight, later)
    sums = []
    for group in (first, later):
        sums.append(group[0])
        sums += [swap(group[j], j) for j in (1, 2, 3)]
    piece, shared = combine(sums, parts, (2, 2))
    pieces = [shared] + [shift(piece, m) for m in (1, 2, 3)]
    other_pieces = [swap(x, 2) for x in pieces]

    own_out, mixed = experts(pieces, gain, weights, None)
    halves = ((2, 1), (3, 0))
    other_out = experts(other_pieces, gain, weights, halves)

    result = 0.0
    for half, out in zip(halves, other_out):
        got = swap(out, 2)
        for at, t in enumerate(half):
            total = own_out[t] + got[at].astype(jnp.float32)
            if t:
                total = shift(total.astype(jnp.bfloat16), -t).astype(jnp.float32)
            result = result + total
    return (mixed, result.astype(jnp.bfloat16))


def body(*args):
    residual, routes = args[3], args[6]
    own_rows, dim = residual.shape
    n_ctx, n_head = lax.axis_size("ctx"), lax.axis_size("head")
    dense = slots_per_expert(own_rows, routes.shape[1], n_ctx * n_head) == own_rows
    dense = dense and n_ctx == 4 and n_head == 4 and (dim // n_ctx) % (2 * HEAD_DIMENSION) == 0
    dense = dense and args[1].shape[1] == HEAD_DIMENSION and n_ctx * n_head <= LANES
    if not dense:
        return sparse_body(*args)
    return dense_body(*args)


def solution(mesh):
    return jax.shard_map(
        body,
        mesh=mesh,
        in_specs=(
            P(("group", "ctx"), "head"),
            P(("group", "ctx"), "head"),
            P(("group", "ctx"), "head"),
            P(("group", "ctx", "head"), None),
            P("head", "ctx"),
            P(),
            P(("group", "ctx", "head"), None),
            P(("group", "ctx", "head"), None),
            P(("ctx", "head"), None, None),
            P(("ctx", "head"), None, None),
            P(("ctx", "head"), None, None),
        ),
        out_specs=(P(("group", "ctx", "head"), None), P(("group", "ctx", "head"), None)),
        check_vma=False,
    )
```

```python
import functools

import jax
import jax.numpy as jnp
from jax import lax
from jax.experimental import pallas as pl
from jax.experimental.pallas import tpu as pltpu
from jax.sharding import PartitionSpec as P


HEAD_DIMENSION = 128
LANES = 64


def expert_apply(arrived, gate_proj, up_proj, down_proj):
    shape_in = arrived.shape
    flat_rows = arrived.reshape(-1, shape_in[-1])
    gate_act = jnp.dot(flat_rows, gate_proj, preferred_element_type=jnp.float32)
    up_act = jnp.dot(flat_rows, up_proj, preferred_element_type=jnp.float32)
    hidden = (jax.nn.silu(gate_act) * up_act).astype(jnp.bfloat16)
    output = jnp.dot(hidden, down_proj, preferred_element_type=jnp.float32).astype(jnp.bfloat16)
    return output.reshape(shape_in)


def sparse_body(query, keys, values, residual, o_weight, gain, routes, gates, w_gate, w_up, w_down):
    head_size = HEAD_DIMENSION
    query_rows = query.shape[0]
    kv_heads = keys.shape[1] // head_size
    q_heads = query.shape[1] // head_size
    head_replicas = q_heads // kv_heads
    scale = head_size ** (-0.5)
    queries = query.reshape(query_rows, kv_heads, head_replicas, head_size)
    first_pos = lax.axis_index("ctx") * query_rows
    query_pos = first_pos + jnp.arange(query_rows, dtype=jnp.int32)
    key_all = lax.all_gather(keys, "ctx", axis=0, tiled=True)
    value_all = lax.all_gather(values, "ctx", axis=0, tiled=True)
    width = key_all.shape[0]
    visible = jnp.arange(width, dtype=jnp.int32)[None, :] <= query_pos[:, None]
    scores = (
        jnp.einsum(
            "veqi,zei->eqvz",
            queries,
            key_all.reshape(width, kv_heads, head_size),
            preferred_element_type=jnp.float32,
        )
        * scale
    )
    scores = jnp.where(visible, scores, -1e30)
    top = jnp.max(scores, axis=-1)
    weights = jnp.where(visible, jnp.exp(scores - top[..., None]), 0.0)
    total = jnp.sum(weights, axis=-1)
    summed_values = jnp.einsum(
        "pexa,apo->pexo",
        weights.astype(jnp.bfloat16),
        value_all.reshape(width, kv_heads, head_size),
        preferred_element_type=jnp.float32,
    )
    attended = (
        (summed_values / total[..., None])
        .transpose(2, 0, 1, 3)
        .reshape(query_rows, q_heads * head_size)
        .astype(jnp.bfloat16)
    )
    head_terms = jnp.dot(
        attended,
        lax.all_gather(o_weight, "ctx", axis=1, tiled=True),
        preferred_element_type=jnp.float32,
    )
    summed = lax.psum_scatter(
        head_terms.astype(jnp.bfloat16), "head", scatter_dimension=0, tiled=True
    ).astype(jnp.float32)
    mixed = (summed + residual.astype(jnp.float32)).astype(jnp.bfloat16)
    mixed_f = mixed.astype(jnp.float32)
    normed = (
        mixed_f * lax.rsqrt(jnp.mean(mixed_f * mixed_f, axis=-1, keepdims=True) + 1e-06) * gain
    ).astype(jnp.bfloat16)
    own_rows = residual.shape[0]
    model_dim = residual.shape[1]
    top_count = routes.shape[1]
    devices = lax.axis_size("ctx") * lax.axis_size("head")
    capacity = slots_per_expert(own_rows, top_count, devices)
    expert_ids = routes.reshape(-1)
    onehot = (expert_ids[:, None] == jnp.arange(devices, dtype=jnp.int32)[None, :]).astype(
        jnp.int32
    )
    slots = jnp.sum((jnp.cumsum(onehot, axis=0) - 1) * onehot, axis=1)
    target = expert_ids * capacity + slots
    outgoing = (
        jnp.zeros((devices * capacity, model_dim), jnp.bfloat16)
        .at[target]
        .set(jnp.repeat(normed, top_count, axis=0))
    )
    outgoing = outgoing.reshape(devices, capacity, model_dim)
    computed = expert_apply(
        lax.all_to_all(outgoing, ("ctx", "head"), split_axis=0, concat_axis=0, tiled=True),
        w_gate[0],
        w_up[0],
        w_down[0],
    )
    returned = lax.all_to_all(computed, ("ctx", "head"), split_axis=0, concat_axis=0, tiled=True)
    selected_entries = returned.reshape(devices * capacity, model_dim)[target]
    selected_entries = selected_entries.astype(jnp.float32).reshape(own_rows, top_count, model_dim)
    weight_norm = gates / jnp.sum(gates, axis=-1, keepdims=True)
    expert_mix = jnp.sum(selected_entries * weight_norm[..., None], axis=1).astype(jnp.bfloat16)
    return (mixed, expert_mix)


def slots_per_expert(own_rows, top_count, devices):
    return min(own_rows, max(2, 2 * own_rows * top_count // devices))


def place():
    return lax.axis_index("ctx"), lax.axis_index("head")


def ring_at(position):
    return position ^ (position >> 1)


def behind(steps):
    n = lax.axis_size("ctx")
    c = lax.axis_index("ctx")
    return ring_at(jnp.bitwise_and(ring_at(c) - steps + n, n - 1))


def shift(x, by):
    n = lax.axis_size("ctx")
    pairs = [(ring_at(i), ring_at((i + by) % n)) for i in range(n)]
    return lax.ppermute(x, "ctx", pairs)


def swap(x, mask):
    n = lax.axis_size("head")
    return lax.ppermute(x, "head", [(i, i ^ mask) for i in range(n)])


def call(kernel, args, out_shape, scratch, flops, moved, limit, fetched=()):
    vmem = pl.BlockSpec(memory_space=pltpu.VMEM)
    away = pl.BlockSpec(memory_space=pltpu.HBM)
    args = [
        pltpu.with_memory_space_constraint(x, pltpu.HBM) if i in fetched else x
        for i, x in enumerate(args)
    ]
    return pl.pallas_call(
        kernel,
        out_shape=out_shape,
        in_specs=[away if i in fetched else vmem for i in range(len(args))],
        out_specs=[vmem] * len(out_shape),
        scratch_shapes=scratch,
        cost_estimate=pl.CostEstimate(flops=flops, bytes_accessed=moved, transcendentals=0),
        compiler_params=pltpu.CompilerParams(vmem_limit_bytes=limit << 20),
    )(*args)


def fetch(pairs, sems):
    copies = [pltpu.make_async_copy(a, b, sems.at[i]) for i, (a, b) in enumerate(pairs)]
    for copy in copies:
        copy.start()
    return copies


def stage_kernel(n, *refs):
    for copy in fetch(tuple(zip(refs[:n], refs[n : 2 * n])), refs[2 * n]):
        copy.wait()


def stage(*arrays):
    n = len(arrays)
    out = [jax.ShapeDtypeStruct(x.shape, x.dtype) for x in arrays]
    scratch = [pltpu.SemaphoreType.DMA((n,))]
    kernel = functools.partial(stage_kernel, n)
    return call(kernel, arrays, out, scratch, 0, 1 << 22, 8, range(n))


def pair_kernel(k_ref, v_ref, out_ref, sems):
    hd = k_ref.shape[1]
    for copy in fetch(((k_ref, out_ref.at[:, :hd]), (v_ref, out_ref.at[:, hd:])), sems):
        copy.wait()


def pair(keys, values):
    out = jax.ShapeDtypeStruct((keys.shape[0], 2 * keys.shape[1]), keys.dtype)
    scratch = [pltpu.SemaphoreType.DMA((2,))]
    return call(pair_kernel, (keys, values), [out], scratch, 0, 1 << 16, 2, (0, 1))[0]


def parts_kernel(n_ctx, skip_in, route_in, gate_in, *refs):
    out_refs, (skip_ref, route_ref, gate_ref, sems) = refs[:n_ctx], refs[n_ctx:]
    copies = fetch(((skip_in, skip_ref), (route_in, route_ref), (gate_in, gate_ref)), sems)
    for copy in copies:
        copy.wait()
    gates = gate_ref[...].T
    routes = route_ref[...].T
    share = gates / jnp.sum(gates, axis=-1, keepdims=True)
    own_rows, dim = skip_ref.shape
    cols = dim // n_ctx
    lanes = lax.broadcasted_iota(jnp.int32, (own_rows, 2 * LANES), 1)
    table = jnp.zeros((own_rows, 2 * LANES), jnp.float32)
    for k in range(gates.shape[1]):
        table += jnp.where(lanes % LANES == routes[:, k : k + 1], share[:, k : k + 1], 0.0)
    high = table.astype(jnp.bfloat16).astype(jnp.float32)
    packed = jnp.where(lanes < LANES, high, table - high).astype(jnp.bfloat16)
    for s, out_ref in enumerate(out_refs):
        at = pl.ds(pl.multiple_of(behind(-s) * cols, cols), cols)
        out_ref[:, :cols] = skip_ref[:, at]
        out_ref[:, cols:] = packed


def make_parts(residual, routes, gates):
    n_ctx = lax.axis_size("ctx")
    own_rows, dim = residual.shape
    part = jax.ShapeDtypeStruct((own_rows, dim // n_ctx + 2 * LANES), jnp.bfloat16)
    args = (residual, routes.T, gates.T)
    scratch = [pltpu.VMEM(x.shape, x.dtype) for x in args] + [pltpu.SemaphoreType.DMA((3,))]
    kernel = functools.partial(parts_kernel, n_ctx)
    return call(kernel, args, [part] * n_ctx, scratch, 0, 1 << 18, 4, (0, 1, 2))


def attend_kernel(steps, splits, n_ctx, n_head, *refs):
    n = len(steps)
    q_refs, refs = refs[: n * splits], refs[n * splits :]
    kv_refs, refs = refs[:n_ctx], refs[n_ctx:]
    w_ref, refs = refs[0], refs[1:]
    keep_ref, send_ref, k_all, v_all, queries, att, prod = refs
    hd = HEAD_DIMENSION
    rows, q_cols = k_all.shape[0] // n_ctx, q_refs[0].shape[1]
    own_rows = rows // n_head
    heads = q_cols // hd
    together = 4
    _, h = place()
    key_pos = []
    for m in range(n_ctx):
        k_all[m * rows : (m + 1) * rows, :] = kv_refs[m][:, :hd]
        v_all[m * rows : (m + 1) * rows, :] = kv_refs[m][:, hd:]
        key_pos.append(behind(m) * rows + lax.broadcasted_iota(jnp.int32, (rows, rows), 1))
    key_pos = jnp.concatenate(key_pos, axis=1)
    row_pos = lax.broadcasted_iota(jnp.int32, (rows, 1), 0)
    scale = hd**-0.5
    for i, step in enumerate(steps):
        visible = key_pos <= behind(step) * rows + row_pos
        for g in range(heads):
            for k, q_ref in enumerate(q_refs[i * splits : (i + 1) * splits]):
                at = g * rows + k * (rows // splits)
                queries[at : at + rows // splits, :] = q_ref[:, g * hd : (g + 1) * hd]
        for g in range(0, heads, together):
            scores = lax.dot_general(
                queries[g * rows : (g + together) * rows, :],
                k_all[...],
                (((1,), (1,)), ((), ())),
                preferred_element_type=jnp.float32,
            ).reshape(together, rows, -1)
            scores = jnp.where(visible[None], scores, -1e30)
            top = jnp.max(scores, axis=-1, keepdims=True)
            weights = jnp.exp((scores - top) * scale)
            total = jnp.sum(weights, axis=-1, keepdims=True)
            summed = jnp.dot(
                weights.astype(jnp.bfloat16).reshape(together * rows, -1),
                v_all[...],
                preferred_element_type=jnp.float32,
            ).reshape(together, rows, hd)
            done = (summed * (1.0 / total)).astype(jnp.bfloat16)
            for k in range(together):
                att[:, (g + k) * hd : (g + k + 1) * hd] = done[k]
        prod[...] = jnp.dot(att[...], w_ref[...], preferred_element_type=jnp.float32)
        for j in range(n_head):
            start = pl.multiple_of(jnp.bitwise_xor(h, j) * own_rows, own_rows)
            block = prod[pl.ds(start, own_rows), :]
            if j % 2:
                send_ref[i, j // 2] = block.astype(jnp.bfloat16)
            else:
                keep_ref[i, j // 2] = block


def attend(steps, q_list, kv_list, o_weight):
    n_ctx, n_head = lax.axis_size("ctx"), lax.axis_size("head")
    rows, q_cols = kv_list[0].shape[0], q_list[0].shape[1]
    out_cols = o_weight.shape[1]
    n = len(steps)
    splits = len(q_list) // n
    piece = (n, n_head // 2, rows // n_head, out_cols)
    out_shape = [jax.ShapeDtypeStruct(piece, t) for t in (jnp.float32, jnp.bfloat16)]
    kernel = functools.partial(attend_kernel, steps, splits, n_ctx, n_head)
    scratch = [
        pltpu.VMEM((rows * n_ctx, HEAD_DIMENSION), jnp.bfloat16),
        pltpu.VMEM((rows * n_ctx, HEAD_DIMENSION), jnp.bfloat16),
        pltpu.VMEM((rows * q_cols // HEAD_DIMENSION, HEAD_DIMENSION), jnp.bfloat16),
        pltpu.VMEM((rows, q_cols), jnp.bfloat16),
        pltpu.VMEM((rows, out_cols), jnp.float32),
    ]
    flops = n * (4 * rows * q_cols * rows * n_ctx + 2 * rows * q_cols * out_cols)
    args = (*q_list, *kv_list, o_weight)
    return call(kernel, args, out_shape, scratch, flops, 2 * q_cols * out_cols, 16)


def halve_kernel(n, *refs):
    keeps, gots, (own_ref, send_ref) = refs[:n], refs[n : 2 * n], refs[2 * n :]
    at = 0
    for keep, got in zip(keeps, gots):
        here = slice(at, at + keep.shape[0])
        total = keep[...] + got[...].astype(jnp.float32)
        own_ref[here] = total[:, 0]
        send_ref[here] = total[:, 1].astype(jnp.bfloat16)
        at += keep.shape[0]


def halve(keeps, gots):
    n_blocks = sum(x.shape[0] for x in keeps)
    shape = (n_blocks, *keeps[0].shape[2:])
    out_shape = [jax.ShapeDtypeStruct(shape, t) for t in (jnp.float32, jnp.bfloat16)]
    kernel = functools.partial(halve_kernel, len(keeps))
    return call(kernel, (*keeps, *gots), out_shape, [], 0, 1 << 20, 6)


def combine_kernel(n_ctx, own_ref, got_ref, *refs):
    part_refs, (piece_ref, shared_ref) = refs[:n_ctx], refs[n_ctx:]
    cols = piece_ref.shape[2]
    for s in range(n_ctx):
        total = own_ref[s] + got_ref[s].astype(jnp.float32)
        block = (total + part_refs[s][:, :cols].astype(jnp.float32)).astype(jnp.bfloat16)
        piece_ref[s] = block
        shared_ref[s, :, :cols] = block
        shared_ref[s, :, cols:] = part_refs[s][:, cols:]


def combine(own, got, parts):
    n_ctx, own_rows, cols = own.shape
    out_shape = [
        jax.ShapeDtypeStruct((n_ctx, own_rows, cols), jnp.bfloat16),
        jax.ShapeDtypeStruct((n_ctx, own_rows, cols + 2 * LANES), jnp.bfloat16),
    ]
    kernel = functools.partial(combine_kernel, n_ctx)
    return call(kernel, (own, got, *parts), out_shape, [], 0, 1 << 20, 4)


def expert_kernel(n_ctx, own, *refs):
    if own:
        pieces, refs = refs[:n_ctx], refs[n_ctx:]
    else:
        shared, near, far, *refs = refs
        pieces = (shared, near.at[0], far, near.at[1])
    gain_ref, refs = refs[0], refs[1:]
    weights, refs = (refs[:3], refs[3:6]), refs[6:]
    outs, (x_ref, acc_ref, share_ref) = refs[:-3], refs[-3:]
    own_rows, cols = pieces[2].shape[1:]
    c, h = place()

    for t in range(n_ctx):
        blocks = []
        square = jnp.zeros((own_rows, 1), jnp.float32)
        for m in range(n_ctx):
            block = pieces[m][(t - m) % n_ctx, :, :cols]
            block_f = block.astype(jnp.float32)
            square += jnp.sum(block_f * block_f, axis=-1, keepdims=True)
            at = pl.ds(pl.multiple_of(behind(m) * cols, cols), cols)
            blocks.append((block_f, at))
            if own and t == 0:
                outs[-1][:, at] = block
        root = lax.rsqrt(square / (cols * n_ctx) + 1e-06)
        here = slice(t * own_rows, (t + 1) * own_rows)
        for block_f, at in blocks:
            x_ref[here, at] = (block_f * root * gain_ref[:, at]).astype(jnp.bfloat16)
        share_ref[here, :] = pieces[0][t, :, cols:].astype(jnp.float32)

    lanes = lax.broadcasted_iota(jnp.int32, share_ref.shape, 1) % LANES
    for i, (gate_ref, up_ref, down_ref) in enumerate(weights):
        expert = c * lax.axis_size("head") + jnp.bitwise_xor(h, i)
        share = jnp.sum(jnp.where(lanes == expert, share_ref[...], 0.0), axis=-1, keepdims=True)
        gate = jnp.dot(x_ref[...], gate_ref[0], preferred_element_type=jnp.float32)
        up = jnp.dot(x_ref[...], up_ref[0], preferred_element_type=jnp.float32)
        hidden = (gate * jax.nn.sigmoid(gate) * up).astype(jnp.bfloat16)
        out = jnp.dot(hidden, down_ref[0], preferred_element_type=jnp.float32) * share
        if i == 0:
            acc_ref[...] = out
        else:
            total = (acc_ref[...] + out).astype(outs[0].dtype)
            for t in range(n_ctx):
                outs[t][...] = total[t * own_rows : (t + 1) * own_rows, :]


def experts(pieces, gain, weights, own):
    n_ctx, own_rows, _ = pieces[0].shape
    _, dim, hidden = weights[0].shape
    rows = own_rows * n_ctx
    out = jax.ShapeDtypeStruct((own_rows, dim), jnp.float32 if own else jnp.bfloat16)
    out_shape = [out] * n_ctx
    if own:
        out_shape.append(jax.ShapeDtypeStruct((own_rows, dim), jnp.bfloat16))
    scratch = [
        pltpu.VMEM((rows, dim), jnp.bfloat16),
        pltpu.VMEM((rows, dim), jnp.float32),
        pltpu.VMEM((rows, 2 * LANES), jnp.float32),
    ]
    args = (*pieces, gain.reshape(1, -1), *weights)
    kernel = functools.partial(expert_kernel, n_ctx, own)
    flops = 12 * rows * dim * hidden
    return call(kernel, args, out_shape, scratch, flops, 12 * dim * hidden, 28)


def add_kernel(a_ref, b_ref, out_ref):
    out_ref[...] = (a_ref[...] + b_ref[...].astype(jnp.float32)).astype(out_ref.dtype)


def add(a, b):
    return call(add_kernel, (a, b), [jax.ShapeDtypeStruct(b.shape, b.dtype)], [], 0, 1 << 19, 2)[0]


def dense_body(query, keys, values, residual, o_weight, gain, routes, gates, w_gate, w_up, w_down):
    q_list = [query]
    for _ in range(3):
        q_list.append(shift(q_list[-1], 1))
    kv = pair(keys, values)
    kv_back = shift(kv, 1)
    kv_list = [kv, kv_back, shift(kv_back, 1), shift(kv, 3)]
    parts = make_parts(residual, routes, gates)
    parts = [parts[0]] + [shift(parts[s], s) for s in (1, 2, 3)]

    weights = [w_gate, w_up, w_down]
    weights += [swap(w, 1) for w in weights]
    o_weight, q_list[0], weights[2] = stage(o_weight, query, w_down)

    first = attend((0, 1, 2), q_list[:3], kv_list, o_weight)
    last = attend((3,), q_list[3:], kv_list, o_weight)
    keeps, sends = zip(first, last)
    gots = [swap(x, 1) for x in sends]
    own, send = halve(keeps, gots)
    piece, shared = combine(own, swap(send, 2), parts)
    back, ahead = shift(piece, 1), shift(piece, 3)
    pieces = [shared, back, shift(back, 1), ahead]
    sides = swap(jnp.stack([back, ahead]), 2)
    other_pieces = [swap(shared, 2), sides, swap(pieces[2], 2)]

    *own_out, mixed = experts(pieces, gain, weights, True)
    other_out = experts(other_pieces, gain, weights, False)

    got = [swap(x, 2) for x in other_out]
    result = own_out[0] + got[0].astype(jnp.float32)
    for t in (1, 2, 3):
        total = shift(add(own_out[t], got[t]), -t)
        result = result + total.astype(jnp.float32)
    return (mixed, result.astype(jnp.bfloat16))


def body(*args):
    residual, routes = args[3], args[6]
    own_rows, dim = residual.shape
    n_ctx, n_head = lax.axis_size("ctx"), lax.axis_size("head")
    dense = slots_per_expert(own_rows, routes.shape[1], n_ctx * n_head) == own_rows
    dense = dense and n_ctx == 4 and n_head == 4 and (dim // n_ctx) % (2 * HEAD_DIMENSION) == 0
    dense = dense and args[1].shape[1] == HEAD_DIMENSION and n_ctx * n_head <= LANES
    if not dense:
        return sparse_body(*args)
    return dense_body(*args)


def solution(mesh):
    return jax.shard_map(
        body,
        mesh=mesh,
        in_specs=(
            P(("group", "ctx"), "head"),
            P(("group", "ctx"), "head"),
            P(("group", "ctx"), "head"),
            P(("group", "ctx", "head"), None),
            P("head", "ctx"),
            P(),
            P(("group", "ctx", "head"), None),
            P(("group", "ctx", "head"), None),
            P(("ctx", "head"), None, None),
            P(("ctx", "head"), None, None),
            P(("ctx", "head"), None, None),
        ),
        out_specs=(P(("group", "ctx", "head"), None), P(("group", "ctx", "head"), None)),
        check_vma=False,
    )
```

```python
import functools

import jax
import jax.numpy as jnp
from jax import lax
from jax.experimental import pallas as pl
from jax.experimental.pallas import tpu as pltpu
from jax.sharding import PartitionSpec as P


HEAD_DIMENSION = 128
LANES = 64


def expert_apply(arrived, gate_proj, up_proj, down_proj):
    shape_in = arrived.shape
    flat_rows = arrived.reshape(-1, shape_in[-1])
    gate_act = jnp.dot(flat_rows, gate_proj, preferred_element_type=jnp.float32)
    up_act = jnp.dot(flat_rows, up_proj, preferred_element_type=jnp.float32)
    hidden = (jax.nn.silu(gate_act) * up_act).astype(jnp.bfloat16)
    output = jnp.dot(hidden, down_proj, preferred_element_type=jnp.float32).astype(jnp.bfloat16)
    return output.reshape(shape_in)


def sparse_body(query, keys, values, residual, o_weight, gain, routes, gates, w_gate, w_up, w_down):
    head_size = HEAD_DIMENSION
    query_rows = query.shape[0]
    kv_heads = keys.shape[1] // head_size
    q_heads = query.shape[1] // head_size
    head_replicas = q_heads // kv_heads
    scale = head_size ** (-0.5)
    queries = query.reshape(query_rows, kv_heads, head_replicas, head_size)
    first_pos = lax.axis_index("ctx") * query_rows
    query_pos = first_pos + jnp.arange(query_rows, dtype=jnp.int32)
    key_all = lax.all_gather(keys, "ctx", axis=0, tiled=True)
    value_all = lax.all_gather(values, "ctx", axis=0, tiled=True)
    width = key_all.shape[0]
    visible = jnp.arange(width, dtype=jnp.int32)[None, :] <= query_pos[:, None]
    scores = (
        jnp.einsum(
            "veqi,zei->eqvz",
            queries,
            key_all.reshape(width, kv_heads, head_size),
            preferred_element_type=jnp.float32,
        )
        * scale
    )
    scores = jnp.where(visible, scores, -1e30)
    top = jnp.max(scores, axis=-1)
    weights = jnp.where(visible, jnp.exp(scores - top[..., None]), 0.0)
    total = jnp.sum(weights, axis=-1)
    summed_values = jnp.einsum(
        "pexa,apo->pexo",
        weights.astype(jnp.bfloat16),
        value_all.reshape(width, kv_heads, head_size),
        preferred_element_type=jnp.float32,
    )
    attended = (
        (summed_values / total[..., None])
        .transpose(2, 0, 1, 3)
        .reshape(query_rows, q_heads * head_size)
        .astype(jnp.bfloat16)
    )
    head_terms = jnp.dot(
        attended,
        lax.all_gather(o_weight, "ctx", axis=1, tiled=True),
        preferred_element_type=jnp.float32,
    )
    summed = lax.psum_scatter(
        head_terms.astype(jnp.bfloat16), "head", scatter_dimension=0, tiled=True
    ).astype(jnp.float32)
    mixed = (summed + residual.astype(jnp.float32)).astype(jnp.bfloat16)
    mixed_f = mixed.astype(jnp.float32)
    normed = (
        mixed_f * lax.rsqrt(jnp.mean(mixed_f * mixed_f, axis=-1, keepdims=True) + 1e-06) * gain
    ).astype(jnp.bfloat16)
    own_rows = residual.shape[0]
    model_dim = residual.shape[1]
    top_count = routes.shape[1]
    devices = lax.axis_size("ctx") * lax.axis_size("head")
    capacity = slots_per_expert(own_rows, top_count, devices)
    expert_ids = routes.reshape(-1)
    onehot = (expert_ids[:, None] == jnp.arange(devices, dtype=jnp.int32)[None, :]).astype(
        jnp.int32
    )
    slots = jnp.sum((jnp.cumsum(onehot, axis=0) - 1) * onehot, axis=1)
    target = expert_ids * capacity + slots
    outgoing = (
        jnp.zeros((devices * capacity, model_dim), jnp.bfloat16)
        .at[target]
        .set(jnp.repeat(normed, top_count, axis=0))
    )
    outgoing = outgoing.reshape(devices, capacity, model_dim)
    computed = expert_apply(
        lax.all_to_all(outgoing, ("ctx", "head"), split_axis=0, concat_axis=0, tiled=True),
        w_gate[0],
        w_up[0],
        w_down[0],
    )
    returned = lax.all_to_all(computed, ("ctx", "head"), split_axis=0, concat_axis=0, tiled=True)
    selected_entries = returned.reshape(devices * capacity, model_dim)[target]
    selected_entries = selected_entries.astype(jnp.float32).reshape(own_rows, top_count, model_dim)
    weight_norm = gates / jnp.sum(gates, axis=-1, keepdims=True)
    expert_mix = jnp.sum(selected_entries * weight_norm[..., None], axis=1).astype(jnp.bfloat16)
    return (mixed, expert_mix)


def slots_per_expert(own_rows, top_count, devices):
    return min(own_rows, max(2, 2 * own_rows * top_count // devices))


def place():
    return lax.axis_index("ctx"), lax.axis_index("head")


def ring_at(position):
    return position ^ (position >> 1)


def behind(steps):
    n = lax.axis_size("ctx")
    c = lax.axis_index("ctx")
    return ring_at(jnp.bitwise_and(ring_at(c) - steps + n, n - 1))


def across(x, mask):
    n = lax.axis_size("ctx")
    return lax.ppermute(x, "ctx", [(i, i ^ mask) for i in range(n)])


def source(m, t):
    n, c = lax.axis_size("ctx"), lax.axis_index("ctx")
    other = jnp.bitwise_xor(c, m)
    return other, jnp.bitwise_and(t - ring_at(c) + ring_at(other) + n, n - 1)


def shift(x, by):
    n = lax.axis_size("ctx")
    pairs = [(ring_at(i), ring_at((i + by) % n)) for i in range(n)]
    return lax.ppermute(x, "ctx", pairs)


def swap(x, mask):
    n = lax.axis_size("head")
    return lax.ppermute(x, "head", [(i, i ^ mask) for i in range(n)])


def call(kernel, args, out_shape, scratch, flops, moved, limit, fetched=()):
    vmem = pl.BlockSpec(memory_space=pltpu.VMEM)
    away = pl.BlockSpec(memory_space=pltpu.HBM)
    args = [
        pltpu.with_memory_space_constraint(x, pltpu.HBM) if i in fetched else x
        for i, x in enumerate(args)
    ]
    return pl.pallas_call(
        kernel,
        out_shape=out_shape,
        in_specs=[away if i in fetched else vmem for i in range(len(args))],
        out_specs=[vmem] * len(out_shape),
        scratch_shapes=scratch,
        cost_estimate=pl.CostEstimate(flops=flops, bytes_accessed=moved, transcendentals=0),
        compiler_params=pltpu.CompilerParams(vmem_limit_bytes=limit << 20),
    )(*args)


def fetch(pairs, sems):
    copies = [pltpu.make_async_copy(a, b, sems.at[i]) for i, (a, b) in enumerate(pairs)]
    for copy in copies:
        copy.start()
    return copies


def stage_kernel(n, *refs):
    for copy in fetch(tuple(zip(refs[:n], refs[n : 2 * n])), refs[2 * n]):
        copy.wait()


def stage(*arrays):
    n = len(arrays)
    out = [jax.ShapeDtypeStruct(x.shape, x.dtype) for x in arrays]
    scratch = [pltpu.SemaphoreType.DMA((n,))]
    kernel = functools.partial(stage_kernel, n)
    return call(kernel, arrays, out, scratch, 0, 1 << 22, 8, range(n))


def pack_kernel(n_ctx, k_in, v_in, skip_in, route_in, gate_in, *refs):
    out_refs, (k_ref, v_ref, skip_ref, route_ref, gate_ref, sems) = refs[:-6], refs[-6:]
    kv_ref, part_refs = out_refs[0], out_refs[1:]
    inputs = (k_in, v_in, skip_in, route_in, gate_in)
    copies = fetch(tuple(zip(inputs, (k_ref, v_ref, skip_ref, route_ref, gate_ref))), sems)
    for copy in copies:
        copy.wait()
    gates = gate_ref[...].T
    routes = route_ref[...].T
    share = gates / jnp.sum(gates, axis=-1, keepdims=True)
    own_rows, dim = skip_ref.shape
    lanes = lax.broadcasted_iota(jnp.int32, (own_rows, 2 * LANES), 1)
    table = jnp.zeros((own_rows, 2 * LANES), jnp.float32)
    for k in range(gates.shape[1]):
        table += jnp.where(lanes % LANES == routes[:, k : k + 1], share[:, k : k + 1], 0.0)
    high = table.astype(jnp.bfloat16).astype(jnp.float32)
    packed = jnp.where(lanes < LANES, high, table - high).astype(jnp.bfloat16)
    hd = HEAD_DIMENSION
    kv_ref[:, :hd] = k_ref[...]
    kv_ref[:, hd:] = v_ref[...]
    rows = k_ref.shape[0]
    for s, out_ref in enumerate(part_refs):
        at = 0
        if s % 2:
            out_ref[:rows, :hd] = k_ref[...]
            out_ref[:rows, hd:] = v_ref[...]
            at = rows
        first = behind(-s) * (dim // n_ctx)
        for i in range(dim // n_ctx // (2 * hd)):
            cols = pl.ds(pl.multiple_of(first + i * 2 * hd, 2 * hd), 2 * hd)
            out_ref[at : at + own_rows, :] = skip_ref[:, cols]
            at += own_rows
        out_ref[at:, : 2 * LANES] = packed[: own_rows // 2]
        out_ref[at:, 2 * LANES :] = packed[own_rows // 2 :]


def part_rows(own_rows, cols):
    return own_rows * cols // (2 * HEAD_DIMENSION) + own_rows // 2


def pack(keys, values, residual, routes, gates):
    n_ctx = lax.axis_size("ctx")
    own_rows, dim = residual.shape
    rows, width = keys.shape[0], 2 * HEAD_DIMENSION
    extra = part_rows(own_rows, dim // n_ctx)
    heights = [rows] + [extra + rows * (s % 2) for s in range(n_ctx)]
    out = [jax.ShapeDtypeStruct((height, width), jnp.bfloat16) for height in heights]
    args = (keys, values, residual, routes.T, gates.T)
    scratch = [pltpu.VMEM(x.shape, x.dtype) for x in args] + [pltpu.SemaphoreType.DMA((5,))]
    kernel = functools.partial(pack_kernel, n_ctx)
    return call(kernel, args, out, scratch, 0, 1 << 18, 4, range(5))


def attend_kernel(steps, splits, n_ctx, n_head, *refs):
    n = len(steps)
    q_refs, refs = refs[: n * splits], refs[n * splits :]
    kv_refs, refs = refs[:n_ctx], refs[n_ctx:]
    w_ref, refs = refs[0], refs[1:]
    keep_ref, send_ref, k_all, v_all, queries, att, prod = refs
    hd = HEAD_DIMENSION
    rows, q_cols = k_all.shape[0] // n_ctx, q_refs[0].shape[1]
    own_rows = rows // n_head
    heads = q_cols // hd
    together = 4
    _, h = place()
    key_pos = []
    for m in range(n_ctx):
        k_all[m * rows : (m + 1) * rows, :] = kv_refs[m][:rows, :hd]
        v_all[m * rows : (m + 1) * rows, :] = kv_refs[m][:rows, hd:]
        key_pos.append(behind(m) * rows + lax.broadcasted_iota(jnp.int32, (rows, rows), 1))
    key_pos = jnp.concatenate(key_pos, axis=1)
    row_pos = lax.broadcasted_iota(jnp.int32, (rows, 1), 0)
    scale = hd**-0.5
    for i, step in enumerate(steps):
        visible = key_pos <= behind(step) * rows + row_pos
        for g in range(heads):
            for k, q_ref in enumerate(q_refs[i * splits : (i + 1) * splits]):
                at = g * rows + k * (rows // splits)
                queries[at : at + rows // splits, :] = q_ref[:, g * hd : (g + 1) * hd]
        for g in range(0, heads, together):
            scores = lax.dot_general(
                queries[g * rows : (g + together) * rows, :],
                k_all[...],
                (((1,), (1,)), ((), ())),
                preferred_element_type=jnp.float32,
            ).reshape(together, rows, -1)
            scores = jnp.where(visible[None], scores, -1e30)
            top = jnp.max(scores, axis=-1, keepdims=True)
            weights = jnp.exp((scores - top) * scale)
            total = jnp.sum(weights, axis=-1, keepdims=True)
            summed = jnp.dot(
                weights.astype(jnp.bfloat16).reshape(together * rows, -1),
                v_all[...],
                preferred_element_type=jnp.float32,
            ).reshape(together, rows, hd)
            done = (summed * (1.0 / total)).astype(jnp.bfloat16)
            for k in range(together):
                att[:, (g + k) * hd : (g + k + 1) * hd] = done[k]
        prod[...] = jnp.dot(att[...], w_ref[...], preferred_element_type=jnp.float32)
        for j in range(n_head):
            start = pl.multiple_of(jnp.bitwise_xor(h, j) * own_rows, own_rows)
            block = prod[pl.ds(start, own_rows), :]
            if j % 2:
                send_ref[i, j // 2] = block.astype(jnp.bfloat16)
            else:
                keep_ref[i, j // 2] = block


def attend(steps, q_list, kv_list, o_weight):
    n_ctx, n_head = lax.axis_size("ctx"), lax.axis_size("head")
    rows, q_cols = kv_list[0].shape[0], q_list[0].shape[1]
    out_cols = o_weight.shape[1]
    n = len(steps)
    splits = len(q_list) // n
    piece = (n, n_head // 2, rows // n_head, out_cols)
    out_shape = [jax.ShapeDtypeStruct(piece, t) for t in (jnp.float32, jnp.bfloat16)]
    kernel = functools.partial(attend_kernel, steps, splits, n_ctx, n_head)
    scratch = [
        pltpu.VMEM((rows * n_ctx, HEAD_DIMENSION), jnp.bfloat16),
        pltpu.VMEM((rows * n_ctx, HEAD_DIMENSION), jnp.bfloat16),
        pltpu.VMEM((rows * q_cols // HEAD_DIMENSION, HEAD_DIMENSION), jnp.bfloat16),
        pltpu.VMEM((rows, q_cols), jnp.bfloat16),
        pltpu.VMEM((rows, out_cols), jnp.float32),
    ]
    flops = n * (4 * rows * q_cols * rows * n_ctx + 2 * rows * q_cols * out_cols)
    args = (*q_list, *kv_list, o_weight)
    return call(kernel, args, out_shape, scratch, flops, 2 * q_cols * out_cols, 16)


def halve_kernel(n, *refs):
    keeps, gots, (own_ref, send_ref) = refs[:n], refs[n : 2 * n], refs[2 * n :]
    at = 0
    for keep, got in zip(keeps, gots):
        here = slice(at, at + keep.shape[0])
        total = keep[...] + got[...].astype(jnp.float32)
        own_ref[here] = total[:, 0]
        send_ref[here] = total[:, 1].astype(jnp.bfloat16)
        at += keep.shape[0]


def halve(keeps, gots):
    n_blocks = sum(x.shape[0] for x in keeps)
    shape = (n_blocks, *keeps[0].shape[2:])
    out_shape = [jax.ShapeDtypeStruct(shape, t) for t in (jnp.float32, jnp.bfloat16)]
    kernel = functools.partial(halve_kernel, len(keeps))
    return call(kernel, (*keeps, *gots), out_shape, [], 0, 1 << 20, 6)


def combine_kernel(n_ctx, own_ref, got_ref, *refs):
    part_refs, (piece_ref, shared_ref) = refs[:n_ctx], refs[n_ctx:]
    own_rows, cols = piece_ref.shape[1:]
    width = part_refs[0].shape[1]
    for s, part_ref in enumerate(part_refs):
        total = own_ref[s] + got_ref[s].astype(jnp.float32)
        at = part_ref.shape[0] - part_rows(own_rows, cols)
        for first in range(0, cols, width):
            here = slice(first, first + width)
            skip = part_ref[at : at + own_rows, :].astype(jnp.float32)
            block = (total[:, here] + skip).astype(jnp.bfloat16)
            piece_ref[s, :, here] = block
            shared_ref[s, :, here] = block
            at += own_rows
        shared_ref[s, : own_rows // 2, cols:] = part_ref[at:, : 2 * LANES]
        shared_ref[s, own_rows // 2 :, cols:] = part_ref[at:, 2 * LANES :]


def combine(own, got, parts):
    n_ctx, own_rows, cols = own.shape
    out_shape = [
        jax.ShapeDtypeStruct((n_ctx, own_rows, cols), jnp.bfloat16),
        jax.ShapeDtypeStruct((n_ctx, own_rows, cols + 2 * LANES), jnp.bfloat16),
    ]
    kernel = functools.partial(combine_kernel, n_ctx)
    return call(kernel, (own, got, *parts), out_shape, [], 0, 1 << 20, 4)


def scaled_piece(piece, m, gain_ref, x_ref):
    n_ctx = piece.shape[0]
    own_rows, cols = x_ref.shape[0] // n_ctx, x_ref.shape[1]
    at = pl.ds(pl.multiple_of(source(m, 0)[0] * cols, cols), cols)
    squares = []
    for t in range(n_ctx):
        block = piece[source(m, t)[1], :, :cols].astype(jnp.float32)
        squares.append(jnp.sum(block * block, axis=-1, keepdims=True))
        x_ref[t * own_rows : (t + 1) * own_rows, :] = (block * gain_ref[:, at]).astype(jnp.bfloat16)
    return jnp.concatenate(squares, axis=0), at


def begin_kernel(early, *refs):
    pieces, (gain_ref, *weights) = refs[:-8], refs[-8:-3]
    acc_ref, square_ref, x_ref = refs[-3:]
    total = 0.0
    rows_of = []
    for k, (m, piece) in enumerate(zip(early, pieces)):
        square, at = scaled_piece(piece, m, gain_ref, x_ref.at[k])
        total += square
        rows_of.append(at)
    square_ref[...] = jnp.broadcast_to(total, square_ref.shape)
    for i, weight in enumerate(weights):
        acc = 0.0
        for k, at in enumerate(rows_of):
            acc += jnp.dot(x_ref[k], weight[0, at, :], preferred_element_type=jnp.float32)
        acc_ref[i] = acc


def begin(pieces, early, gain, weights):
    n_ctx, own_rows, cols = pieces[1].shape
    rows = n_ctx * own_rows
    _, dim, hidden = weights[0].shape
    args = (*pieces, gain, weights[0], weights[1], weights[3], weights[4])
    out_shape = [
        jax.ShapeDtypeStruct((4, rows, hidden), jnp.float32),
        jax.ShapeDtypeStruct((rows, 2 * LANES), jnp.float32),
    ]
    scratch = [pltpu.VMEM((len(early), rows, cols), jnp.bfloat16)]
    kernel = functools.partial(begin_kernel, early)
    flops = 8 * rows * len(early) * cols * hidden
    return call(kernel, args, out_shape, scratch, flops, 8 * dim * hidden, 24)


def finish_kernel(late, n_ctx, own, *refs):
    pieces, refs = refs[:n_ctx], refs[n_ctx:]
    acc_ref, square_ref, gain_ref, *refs = refs
    weights, refs = (refs[:3], refs[3:6]), refs[6:]
    outs, (x_ref, out_ref, share_ref) = refs[:-3], refs[-3:]
    cols = x_ref.shape[1]
    own_rows = x_ref.shape[0] // n_ctx
    c, h = place()
    square, at = scaled_piece(pieces[late], late, gain_ref, x_ref)
    root = lax.rsqrt((square + square_ref[:, :1]) / (cols * n_ctx) + 1e-06)
    if own:
        for m in range(n_ctx):
            column, place_0 = source(m, 0)
            here = pl.ds(pl.multiple_of(column * cols, cols), cols)
            outs[-1][:, here] = pieces[m][place_0, :, :cols]
    for t in range(n_ctx):
        here = slice(t * own_rows, (t + 1) * own_rows)
        share_ref[here, :] = pieces[0][t, :, cols:].astype(jnp.float32)
    lanes = lax.broadcasted_iota(jnp.int32, share_ref.shape, 1) % LANES
    for i, (gate_ref, up_ref, down_ref) in enumerate(weights):
        expert = c * lax.axis_size("head") + jnp.bitwise_xor(h, i)
        share = jnp.sum(jnp.where(lanes == expert, share_ref[...], 0.0), axis=-1, keepdims=True)
        gate, up = (
            (
                acc_ref[2 * i + k]
                + jnp.dot(x_ref[...], ref[0, at, :], preferred_element_type=jnp.float32)
            )
            * root
            for k, ref in enumerate((gate_ref, up_ref))
        )
        hidden = (gate * jax.nn.sigmoid(gate) * up).astype(jnp.bfloat16)
        out = jnp.dot(hidden, down_ref[0], preferred_element_type=jnp.float32) * share
        if i == 0:
            out_ref[...] = out
        else:
            total = (out_ref[...] + out).astype(outs[0].dtype)
            for t in range(n_ctx):
                outs[t][...] = total[t * own_rows : (t + 1) * own_rows, :]


def finish(pieces, late, begun, gain, weights, own):
    n_ctx, own_rows, cols = pieces[1].shape
    _, dim, hidden = weights[0].shape
    rows = own_rows * n_ctx
    out = jax.ShapeDtypeStruct((own_rows, dim), jnp.float32 if own else jnp.bfloat16)
    out_shape = [out] * n_ctx
    if own:
        out_shape.append(jax.ShapeDtypeStruct((own_rows, dim), jnp.bfloat16))
    scratch = [
        pltpu.VMEM((rows, cols), jnp.bfloat16),
        pltpu.VMEM((rows, dim), jnp.float32),
        pltpu.VMEM((rows, 2 * LANES), jnp.float32),
    ]
    args = (*pieces, *begun, gain, *weights)
    kernel = functools.partial(finish_kernel, late, n_ctx, own)
    flops = 4 * rows * hidden * (2 * cols + dim)
    return call(kernel, args, out_shape, scratch, flops, 12 * dim * hidden, 28)


def add_kernel(a_ref, b_ref, out_ref):
    out_ref[...] = (a_ref[...] + b_ref[...].astype(jnp.float32)).astype(out_ref.dtype)


def add(a, b):
    return call(add_kernel, (a, b), [jax.ShapeDtypeStruct(b.shape, b.dtype)], [], 0, 1 << 19, 2)[0]


def dense_body(query, keys, values, residual, o_weight, gain, routes, gates, w_gate, w_up, w_down):
    q_list = [query]
    for _ in range(3):
        q_list.append(shift(q_list[-1], 1))
    kv, *parts = pack(keys, values, residual, routes, gates)
    parts = [parts[0]] + [shift(parts[s], s) for s in (1, 2, 3)]
    kv_list = [kv, parts[1], shift(parts[1][: kv.shape[0]], 1), parts[3]]

    weights = [w_gate, w_up, w_down]
    weights += [swap(w, 1) for w in weights]
    o_weight, q_list[0], weights[2] = stage(o_weight, query, w_down)

    first = attend((0, 1, 2), q_list[:3], kv_list, o_weight)
    last = attend((3,), q_list[3:], kv_list, o_weight)
    keeps, sends = zip(first, last)
    gots = [swap(x, 1) for x in sends]
    own, send = halve(keeps, gots)
    piece, shared = combine(own, swap(send, 2), parts)
    pieces = [shared, across(piece, 1), across(piece, 2)]
    pieces.append(across(pieces[2], 1))
    other_pieces = [swap(x, 2) for x in pieces]

    gain = gain.reshape(1, -1)
    early, late = (0, 1, 2), 3
    own_begun = begin(pieces[:late], early, gain, weights)
    *own_out, mixed = finish(pieces, late, own_begun, gain, weights, True)
    other_begun = begin(other_pieces[:late], early, gain, weights)
    other_out = finish(other_pieces, late, other_begun, gain, weights, False)

    got = [swap(x, 2) for x in other_out]
    result = own_out[0] + got[0].astype(jnp.float32)
    for t in (1, 2, 3):
        total = shift(add(own_out[t], got[t]), -t)
        result = result + total.astype(jnp.float32)
    return (mixed, result.astype(jnp.bfloat16))


def body(*args):
    residual, routes = args[3], args[6]
    own_rows, dim = residual.shape
    n_ctx, n_head = lax.axis_size("ctx"), lax.axis_size("head")
    dense = slots_per_expert(own_rows, routes.shape[1], n_ctx * n_head) == own_rows
    dense = dense and n_ctx == 4 and n_head == 4 and (dim // n_ctx) % (2 * HEAD_DIMENSION) == 0
    dense = dense and 4 * LANES == 2 * HEAD_DIMENSION and own_rows % 32 == 0
    dense = dense and args[1].shape[1] == HEAD_DIMENSION and n_ctx * n_head <= LANES
    if not dense:
        return sparse_body(*args)
    return dense_body(*args)


def solution(mesh):
    return jax.shard_map(
        body,
        mesh=mesh,
        in_specs=(
            P(("group", "ctx"), "head"),
            P(("group", "ctx"), "head"),
            P(("group", "ctx"), "head"),
            P(("group", "ctx", "head"), None),
            P("head", "ctx"),
            P(),
            P(("group", "ctx", "head"), None),
            P(("group", "ctx", "head"), None),
            P(("ctx", "head"), None, None),
            P(("ctx", "head"), None, None),
            P(("ctx", "head"), None, None),
        ),
        out_specs=(P(("group", "ctx", "head"), None), P(("group", "ctx", "head"), None)),
        check_vma=False,
    )
```

```python
import functools
import math

import jax
import jax.numpy as jnp
from jax import lax
from jax.experimental import pallas as pl
from jax.experimental.pallas import tpu as pltpu
from jax.sharding import PartitionSpec as P


HEAD_DIMENSION = 128
LANES = 64


def expert_apply(arrived, gate_proj, up_proj, down_proj):
    shape_in = arrived.shape
    flat_rows = arrived.reshape(-1, shape_in[-1])
    gate_act = jnp.dot(flat_rows, gate_proj, preferred_element_type=jnp.float32)
    up_act = jnp.dot(flat_rows, up_proj, preferred_element_type=jnp.float32)
    hidden = (jax.nn.silu(gate_act) * up_act).astype(jnp.bfloat16)
    output = jnp.dot(hidden, down_proj, preferred_element_type=jnp.float32).astype(jnp.bfloat16)
    return output.reshape(shape_in)


def sparse_body(query, keys, values, residual, o_weight, gain, routes, gates, w_gate, w_up, w_down):
    head_size = HEAD_DIMENSION
    query_rows = query.shape[0]
    kv_heads = keys.shape[1] // head_size
    q_heads = query.shape[1] // head_size
    head_replicas = q_heads // kv_heads
    scale = head_size ** (-0.5)
    queries = query.reshape(query_rows, kv_heads, head_replicas, head_size)
    first_pos = lax.axis_index("ctx") * query_rows
    query_pos = first_pos + jnp.arange(query_rows, dtype=jnp.int32)
    key_all = lax.all_gather(keys, "ctx", axis=0, tiled=True)
    value_all = lax.all_gather(values, "ctx", axis=0, tiled=True)
    width = key_all.shape[0]
    visible = jnp.arange(width, dtype=jnp.int32)[None, :] <= query_pos[:, None]
    scores = (
        jnp.einsum(
            "veqi,zei->eqvz",
            queries,
            key_all.reshape(width, kv_heads, head_size),
            preferred_element_type=jnp.float32,
        )
        * scale
    )
    scores = jnp.where(visible, scores, -1e30)
    top = jnp.max(scores, axis=-1)
    weights = jnp.where(visible, jnp.exp(scores - top[..., None]), 0.0)
    total = jnp.sum(weights, axis=-1)
    summed_values = jnp.einsum(
        "pexa,apo->pexo",
        weights.astype(jnp.bfloat16),
        value_all.reshape(width, kv_heads, head_size),
        preferred_element_type=jnp.float32,
    )
    attended = (
        (summed_values / total[..., None])
        .transpose(2, 0, 1, 3)
        .reshape(query_rows, q_heads * head_size)
        .astype(jnp.bfloat16)
    )
    head_terms = jnp.dot(
        attended,
        lax.all_gather(o_weight, "ctx", axis=1, tiled=True),
        preferred_element_type=jnp.float32,
    )
    summed = lax.psum_scatter(
        head_terms.astype(jnp.bfloat16), "head", scatter_dimension=0, tiled=True
    ).astype(jnp.float32)
    mixed = (summed + residual.astype(jnp.float32)).astype(jnp.bfloat16)
    mixed_f = mixed.astype(jnp.float32)
    normed = (
        mixed_f * lax.rsqrt(jnp.mean(mixed_f * mixed_f, axis=-1, keepdims=True) + 1e-06) * gain
    ).astype(jnp.bfloat16)
    own_rows = residual.shape[0]
    model_dim = residual.shape[1]
    top_count = routes.shape[1]
    devices = lax.axis_size("ctx") * lax.axis_size("head")
    capacity = slots_per_expert(own_rows, top_count, devices)
    expert_ids = routes.reshape(-1)
    onehot = (expert_ids[:, None] == jnp.arange(devices, dtype=jnp.int32)[None, :]).astype(
        jnp.int32
    )
    slots = jnp.sum((jnp.cumsum(onehot, axis=0) - 1) * onehot, axis=1)
    target = expert_ids * capacity + slots
    outgoing = (
        jnp.zeros((devices * capacity, model_dim), jnp.bfloat16)
        .at[target]
        .set(jnp.repeat(normed, top_count, axis=0))
    )
    outgoing = outgoing.reshape(devices, capacity, model_dim)
    computed = expert_apply(
        lax.all_to_all(outgoing, ("ctx", "head"), split_axis=0, concat_axis=0, tiled=True),
        w_gate[0],
        w_up[0],
        w_down[0],
    )
    returned = lax.all_to_all(computed, ("ctx", "head"), split_axis=0, concat_axis=0, tiled=True)
    selected_entries = returned.reshape(devices * capacity, model_dim)[target]
    selected_entries = selected_entries.astype(jnp.float32).reshape(own_rows, top_count, model_dim)
    weight_norm = gates / jnp.sum(gates, axis=-1, keepdims=True)
    expert_mix = jnp.sum(selected_entries * weight_norm[..., None], axis=1).astype(jnp.bfloat16)
    return (mixed, expert_mix)


def slots_per_expert(own_rows, top_count, devices):
    return min(own_rows, max(2, 2 * own_rows * top_count // devices))


def place():
    return lax.axis_index("ctx"), lax.axis_index("head")


def ring_at(position):
    return position ^ (position >> 1)


def behind(steps):
    n = lax.axis_size("ctx")
    c = lax.axis_index("ctx")
    return ring_at(jnp.bitwise_and(ring_at(c) - steps + n, n - 1))


def across(x, mask):
    n = lax.axis_size("ctx")
    return lax.ppermute(x, "ctx", [(i, i ^ mask) for i in range(n)])


def source(m, t):
    n, c = lax.axis_size("ctx"), lax.axis_index("ctx")
    other, owner = jnp.bitwise_xor(c, m), jnp.bitwise_xor(c, t)
    return other, jnp.bitwise_and(ring_at(other) - ring_at(owner) + n, n - 1)


def shift(x, by):
    n = lax.axis_size("ctx")
    pairs = [(ring_at(i), ring_at((i + by) % n)) for i in range(n)]
    return lax.ppermute(x, "ctx", pairs)


def swap(x, mask):
    n = lax.axis_size("head")
    return lax.ppermute(x, "head", [(i, i ^ mask) for i in range(n)])


def call(kernel, args, out_shape, scratch, flops, moved, limit, fetched=()):
    vmem = pl.BlockSpec(memory_space=pltpu.VMEM)
    away = pl.BlockSpec(memory_space=pltpu.HBM)
    args = [
        pltpu.with_memory_space_constraint(x, pltpu.HBM) if i in fetched else x
        for i, x in enumerate(args)
    ]
    return pl.pallas_call(
        kernel,
        out_shape=out_shape,
        in_specs=[away if i in fetched else vmem for i in range(len(args))],
        out_specs=[vmem] * len(out_shape),
        scratch_shapes=scratch,
        cost_estimate=pl.CostEstimate(flops=flops, bytes_accessed=moved, transcendentals=0),
        compiler_params=pltpu.CompilerParams(vmem_limit_bytes=limit << 20),
    )(*args)


def fetch(pairs, sems):
    copies = [pltpu.make_async_copy(a, b, sems.at[i]) for i, (a, b) in enumerate(pairs)]
    for copy in copies:
        copy.start()
    return copies


def stage_kernel(n, *refs):
    for copy in fetch(tuple(zip(refs[:n], refs[n : 2 * n])), refs[2 * n]):
        copy.wait()


def stage(*arrays):
    n = len(arrays)
    out = [jax.ShapeDtypeStruct(x.shape, x.dtype) for x in arrays]
    scratch = [pltpu.SemaphoreType.DMA((n,))]
    kernel = functools.partial(stage_kernel, n)
    return call(kernel, arrays, out, scratch, 0, 1 << 22, 8, range(n))


def pack_kernel(n_ctx, k_in, v_in, skip_in, route_in, gate_in, *refs):
    out_refs, (k_ref, v_ref, skip_ref, route_ref, gate_ref, sems) = refs[:-6], refs[-6:]
    kv_ref, part_refs = out_refs[0], out_refs[1:]
    inputs = (k_in, v_in, skip_in, route_in, gate_in)
    copies = fetch(tuple(zip(inputs, (k_ref, v_ref, skip_ref, route_ref, gate_ref))), sems)
    for copy in copies:
        copy.wait()
    gates = gate_ref[...].T
    routes = route_ref[...].T
    share = gates / jnp.sum(gates, axis=-1, keepdims=True)
    own_rows, dim = skip_ref.shape
    lanes = lax.broadcasted_iota(jnp.int32, (own_rows, 2 * LANES), 1)
    table = jnp.zeros((own_rows, 2 * LANES), jnp.float32)
    for k in range(gates.shape[1]):
        table += jnp.where(lanes % LANES == routes[:, k : k + 1], share[:, k : k + 1], 0.0)
    high = table.astype(jnp.bfloat16).astype(jnp.float32)
    packed = jnp.where(lanes < LANES, high, table - high).astype(jnp.bfloat16)
    hd = HEAD_DIMENSION
    kv_ref[:, :hd] = k_ref[...]
    kv_ref[:, hd:] = v_ref[...]
    rows = k_ref.shape[0]
    for s, out_ref in enumerate(part_refs):
        at = 0
        if s % 2:
            out_ref[:rows, :hd] = k_ref[...]
            out_ref[:rows, hd:] = v_ref[...]
            at = rows
        first = behind(-s) * (dim // n_ctx)
        for i in range(dim // n_ctx // (2 * hd)):
            cols = pl.ds(pl.multiple_of(first + i * 2 * hd, 2 * hd), 2 * hd)
            out_ref[at : at + own_rows, :] = skip_ref[:, cols]
            at += own_rows
        out_ref[at:, : 2 * LANES] = packed[: own_rows // 2]
        out_ref[at:, 2 * LANES :] = packed[own_rows // 2 :]


def part_rows(own_rows, cols):
    return own_rows * cols // (2 * HEAD_DIMENSION) + own_rows // 2


def pack(keys, values, residual, routes, gates):
    n_ctx = lax.axis_size("ctx")
    own_rows, dim = residual.shape
    rows, width = keys.shape[0], 2 * HEAD_DIMENSION
    extra = part_rows(own_rows, dim // n_ctx)
    heights = [rows] + [extra + rows * (s % 2) for s in range(n_ctx)]
    out = [jax.ShapeDtypeStruct((height, width), jnp.bfloat16) for height in heights]
    args = (keys, values, residual, routes.T, gates.T)
    scratch = [pltpu.VMEM(x.shape, x.dtype) for x in args] + [pltpu.SemaphoreType.DMA((5,))]
    kernel = functools.partial(pack_kernel, n_ctx)
    return call(kernel, args, out, scratch, 0, 1 << 18, 4, range(5))


def attend_kernel(steps, splits, n_ctx, n_head, *refs):
    n = len(steps)
    q_refs, refs = refs[: n * splits], refs[n * splits :]
    kv_refs, refs = refs[:n_ctx], refs[n_ctx:]
    w_ref, refs = refs[0], refs[1:]
    keep_ref, send_ref, k_all, v_all, queries, att, prod = refs
    hd = HEAD_DIMENSION
    rows, q_cols = k_all.shape[0] // n_ctx, q_refs[0].shape[1]
    own_rows = rows // n_head
    heads = q_cols // hd
    together = 4
    _, h = place()
    key_pos = []
    for m in range(n_ctx):
        k_all[m * rows : (m + 1) * rows, :] = kv_refs[m][:rows, :hd]
        v_all[m * rows : (m + 1) * rows, :] = kv_refs[m][:rows, hd:]
        key_pos.append(behind(m) * rows + lax.broadcasted_iota(jnp.int32, (rows, rows), 1))
    key_pos = jnp.concatenate(key_pos, axis=1)
    row_pos = lax.broadcasted_iota(jnp.int32, (rows, 1), 0)
    scale = hd**-0.5
    for i, step in enumerate(steps):
        visible = key_pos <= behind(step) * rows + row_pos
        for g in range(heads):
            for k, q_ref in enumerate(q_refs[i * splits : (i + 1) * splits]):
                at = g * rows + k * (rows // splits)
                queries[at : at + rows // splits, :] = q_ref[:, g * hd : (g + 1) * hd]
        for g in range(0, heads, together):
            scores = lax.dot_general(
                queries[g * rows : (g + together) * rows, :],
                k_all[...],
                (((1,), (1,)), ((), ())),
                preferred_element_type=jnp.float32,
            ).reshape(together, rows, -1)
            scores = jnp.where(visible[None], scores, -1e30)
            top = jnp.max(scores, axis=-1, keepdims=True)
            weights = jnp.exp2((scores - top) * (scale * math.log2(math.e)))
            total = jnp.sum(weights, axis=-1, keepdims=True)
            summed = jnp.dot(
                weights.astype(jnp.bfloat16).reshape(together * rows, -1),
                v_all[...],
                preferred_element_type=jnp.float32,
            ).reshape(together, rows, hd)
            done = (summed * (1.0 / total)).astype(jnp.bfloat16)
            for k in range(together):
                att[:, (g + k) * hd : (g + k + 1) * hd] = done[k]
        prod[...] = jnp.dot(att[...], w_ref[...], preferred_element_type=jnp.float32)
        for j in range(n_head):
            start = pl.multiple_of(jnp.bitwise_xor(h, j) * own_rows, own_rows)
            block = prod[pl.ds(start, own_rows), :]
            if j % 2:
                send_ref[i, j // 2] = block.astype(jnp.bfloat16)
            else:
                keep_ref[i, j // 2] = block


def attend(steps, q_list, kv_list, o_weight):
    n_ctx, n_head = lax.axis_size("ctx"), lax.axis_size("head")
    rows, q_cols = kv_list[0].shape[0], q_list[0].shape[1]
    out_cols = o_weight.shape[1]
    n = len(steps)
    splits = len(q_list) // n
    piece = (n, n_head // 2, rows // n_head, out_cols)
    out_shape = [jax.ShapeDtypeStruct(piece, t) for t in (jnp.float32, jnp.bfloat16)]
    kernel = functools.partial(attend_kernel, steps, splits, n_ctx, n_head)
    scratch = [
        pltpu.VMEM((rows * n_ctx, HEAD_DIMENSION), jnp.bfloat16),
        pltpu.VMEM((rows * n_ctx, HEAD_DIMENSION), jnp.bfloat16),
        pltpu.VMEM((rows * q_cols // HEAD_DIMENSION, HEAD_DIMENSION), jnp.bfloat16),
        pltpu.VMEM((rows, q_cols), jnp.bfloat16),
        pltpu.VMEM((rows, out_cols), jnp.float32),
    ]
    flops = n * (4 * rows * q_cols * rows * n_ctx + 2 * rows * q_cols * out_cols)
    args = (*q_list, *kv_list, o_weight)
    return call(kernel, args, out_shape, scratch, flops, 2 * q_cols * out_cols, 16)


def halve_kernel(keep_ref, got_ref, own_ref, send_ref):
    total = keep_ref[...] + got_ref[...].astype(jnp.float32)
    own_ref[...] = total[:, 0]
    send_ref[...] = total[:, 1].astype(jnp.bfloat16)


def halve(keep, got):
    shape = (keep.shape[0], *keep.shape[2:])
    out_shape = [jax.ShapeDtypeStruct(shape, t) for t in (jnp.float32, jnp.bfloat16)]
    return call(halve_kernel, (keep, got), out_shape, [], 0, 1 << 20, 6)


def combine_kernel(n_ctx, n, *refs):
    owns, gots, refs = refs[:n], refs[n : 2 * n], refs[2 * n :]
    part_refs, (piece_ref, shared_ref) = refs[:n_ctx], refs[n_ctx:]
    own_rows, cols = piece_ref.shape[1:]
    width = part_refs[0].shape[1]
    blocks = [(own, got, i) for own, got in zip(owns, gots) for i in range(own.shape[0])]
    for s, ((own, got, i), part_ref) in enumerate(zip(blocks, part_refs)):
        total = own[i] + got[i].astype(jnp.float32)
        at = part_ref.shape[0] - part_rows(own_rows, cols)
        for first in range(0, cols, width):
            here = slice(first, first + width)
            skip = part_ref[at : at + own_rows, :].astype(jnp.float32)
            block = (total[:, here] + skip).astype(jnp.bfloat16)
            piece_ref[s, :, here] = block
            shared_ref[s, :, here] = block
            at += own_rows
        shared_ref[s, : own_rows // 2, cols:] = part_ref[at:, : 2 * LANES]
        shared_ref[s, own_rows // 2 :, cols:] = part_ref[at:, 2 * LANES :]


def combine(owns, gots, parts):
    n_ctx = len(parts)
    _, own_rows, cols = owns[0].shape
    out_shape = [
        jax.ShapeDtypeStruct((n_ctx, own_rows, cols), jnp.bfloat16),
        jax.ShapeDtypeStruct((n_ctx, own_rows, cols + 2 * LANES), jnp.bfloat16),
    ]
    kernel = functools.partial(combine_kernel, n_ctx, len(owns))
    return call(kernel, (*owns, *gots, *parts), out_shape, [], 0, 1 << 20, 4)


def scaled_piece(piece, m, gain_ref, x_ref):
    n_ctx = piece.shape[0]
    own_rows, cols = x_ref.shape[0] // n_ctx, x_ref.shape[1]
    at = pl.ds(pl.multiple_of(source(m, 0)[0] * cols, cols), cols)
    squares = []
    for t in range(n_ctx):
        block = piece[source(m, t)[1], :, :cols].astype(jnp.float32)
        squares.append(jnp.sum(block * block, axis=-1, keepdims=True))
        x_ref[t * own_rows : (t + 1) * own_rows, :] = (block * gain_ref[:, at]).astype(jnp.bfloat16)
    return jnp.concatenate(squares, axis=0), at


def begin_kernel(early, *refs):
    pieces, (gain_ref, *weights) = refs[:-8], refs[-8:-3]
    acc_ref, square_ref, x_ref = refs[-3:]
    total = 0.0
    rows_of = []
    for k, (m, piece) in enumerate(zip(early, pieces)):
        square, at = scaled_piece(piece, m, gain_ref, x_ref.at[k])
        total += square
        rows_of.append(at)
    square_ref[...] = jnp.broadcast_to(total, square_ref.shape)
    for i, weight in enumerate(weights):
        acc = 0.0
        for k, at in enumerate(rows_of):
            acc += jnp.dot(x_ref[k], weight[0, at, :], preferred_element_type=jnp.float32)
        acc_ref[i] = acc


def begin(pieces, early, gain, weights):
    n_ctx, own_rows, cols = pieces[1].shape
    rows = n_ctx * own_rows
    _, dim, hidden = weights[0].shape
    args = (*pieces, gain, weights[0], weights[1], weights[3], weights[4])
    out_shape = [
        jax.ShapeDtypeStruct((4, rows, hidden), jnp.float32),
        jax.ShapeDtypeStruct((rows, 2 * LANES), jnp.float32),
    ]
    scratch = [pltpu.VMEM((len(early), rows, cols), jnp.bfloat16)]
    kernel = functools.partial(begin_kernel, early)
    flops = 8 * rows * len(early) * cols * hidden
    return call(kernel, args, out_shape, scratch, flops, 8 * dim * hidden, 24)


def finish_kernel(late, n_ctx, own, *refs):
    pieces, refs = refs[:n_ctx], refs[n_ctx:]
    acc_ref, square_ref, gain_ref, *refs = refs
    weights, refs = (refs[:3], refs[3:6]), refs[6:]
    outs, (x_ref, out_ref, share_ref) = refs[:-3], refs[-3:]
    cols = x_ref.shape[1]
    own_rows = x_ref.shape[0] // n_ctx
    c, h = place()
    square, at = scaled_piece(pieces[late], late, gain_ref, x_ref)
    root = lax.rsqrt((square + square_ref[:, :1]) / (cols * n_ctx) + 1e-06)
    if own:
        for m in range(n_ctx):
            column, place_0 = source(m, 0)
            here = pl.ds(pl.multiple_of(column * cols, cols), cols)
            outs[-1][:, here] = pieces[m][place_0, :, :cols]
    for t in range(n_ctx):
        here = slice(t * own_rows, (t + 1) * own_rows)
        share_ref[here, :] = pieces[0][source(0, t)[1], :, cols:].astype(jnp.float32)
    lanes = lax.broadcasted_iota(jnp.int32, share_ref.shape, 1) % LANES
    for i, (gate_ref, up_ref, down_ref) in enumerate(weights):
        expert = c * lax.axis_size("head") + jnp.bitwise_xor(h, i)
        share = jnp.sum(jnp.where(lanes == expert, share_ref[...], 0.0), axis=-1, keepdims=True)
        gate, up = (
            (
                acc_ref[2 * i + k]
                + jnp.dot(x_ref[...], ref[0, at, :], preferred_element_type=jnp.float32)
            )
            * root
            for k, ref in enumerate((gate_ref, up_ref))
        )
        hidden = (gate * jax.nn.sigmoid(gate) * up).astype(jnp.bfloat16)
        out = jnp.dot(hidden, down_ref[0], preferred_element_type=jnp.float32) * share
        if i == 0:
            out_ref[...] = out
        else:
            total = (out_ref[...] + out).astype(outs[0].dtype)
            for t in range(n_ctx):
                outs[t][...] = total[t * own_rows : (t + 1) * own_rows, :]


def finish(pieces, late, begun, gain, weights, own):
    n_ctx, own_rows, cols = pieces[1].shape
    _, dim, hidden = weights[0].shape
    rows = own_rows * n_ctx
    out = jax.ShapeDtypeStruct((own_rows, dim), jnp.float32 if own else jnp.bfloat16)
    out_shape = [out] * n_ctx
    if own:
        out_shape.append(jax.ShapeDtypeStruct((own_rows, dim), jnp.bfloat16))
    scratch = [
        pltpu.VMEM((rows, cols), jnp.bfloat16),
        pltpu.VMEM((rows, dim), jnp.float32),
        pltpu.VMEM((rows, 2 * LANES), jnp.float32),
    ]
    args = (*pieces, *begun, gain, *weights)
    kernel = functools.partial(finish_kernel, late, n_ctx, own)
    flops = 4 * rows * hidden * (2 * cols + dim)
    return call(kernel, args, out_shape, scratch, flops, 12 * dim * hidden, 28)


def add_kernel(a_ref, b_ref, out_ref):
    out_ref[...] = (a_ref[...] + b_ref[...].astype(jnp.float32)).astype(out_ref.dtype)


def add(a, b):
    return call(add_kernel, (a, b), [jax.ShapeDtypeStruct(b.shape, b.dtype)], [], 0, 1 << 19, 2)[0]


def dense_body(query, keys, values, residual, o_weight, gain, routes, gates, w_gate, w_up, w_down):
    q_list = [query]
    for _ in range(3):
        q_list.append(shift(q_list[-1], 1))
    kv, *parts = pack(keys, values, residual, routes, gates)
    parts = [parts[0]] + [shift(parts[s], s) for s in (1, 2, 3)]
    kv_list = [kv, parts[1], shift(parts[1][: kv.shape[0]], 1), parts[3]]

    weights = [w_gate, w_up, w_down]
    weights += [swap(w, 1) for w in weights]
    o_weight, q_list[0], weights[2] = stage(o_weight, query, w_down)

    first = attend((0, 1, 2), q_list[:3], kv_list, o_weight)
    last = attend((3,), q_list[3:], kv_list, o_weight)
    keeps, sends = zip(first, last)
    owns, gots = [], []
    for keep, send in zip(keeps, sends):
        own, send = halve(keep, swap(send, 1))
        owns.append(own)
        gots.append(swap(send, 2))
    piece, shared = combine(owns, gots, parts)
    pieces = [shared, across(piece, 1), across(piece, 2)]
    pieces.append(across(pieces[2], 1))
    other_pieces = [swap(x, 2) for x in pieces]

    gain = gain.reshape(1, -1)
    early, late = (0, 1, 2), 3
    own_begun = begin(pieces[:late], early, gain, weights)
    *own_out, mixed = finish(pieces, late, own_begun, gain, weights, True)
    other_begun = begin(other_pieces[:late], early, gain, weights)
    other_out = finish(other_pieces, late, other_begun, gain, weights, False)

    got = [swap(x, 2) for x in other_out]
    result = own_out[0] + got[0].astype(jnp.float32)
    for t in (1, 2, 3):
        total = across(add(own_out[t], got[t]), t)
        result = result + total.astype(jnp.float32)
    return (mixed, result.astype(jnp.bfloat16))


def body(*args):
    residual, routes = args[3], args[6]
    own_rows, dim = residual.shape
    n_ctx, n_head = lax.axis_size("ctx"), lax.axis_size("head")
    dense = slots_per_expert(own_rows, routes.shape[1], n_ctx * n_head) == own_rows
    dense = dense and n_ctx == 4 and n_head == 4 and (dim // n_ctx) % (2 * HEAD_DIMENSION) == 0
    dense = dense and 4 * LANES == 2 * HEAD_DIMENSION and own_rows % 32 == 0
    dense = dense and args[1].shape[1] == HEAD_DIMENSION and n_ctx * n_head <= LANES
    if not dense:
        return sparse_body(*args)
    return dense_body(*args)


def solution(mesh):
    return jax.shard_map(
        body,
        mesh=mesh,
        in_specs=(
            P(("group", "ctx"), "head"),
            P(("group", "ctx"), "head"),
            P(("group", "ctx"), "head"),
            P(("group", "ctx", "head"), None),
            P("head", "ctx"),
            P(),
            P(("group", "ctx", "head"), None),
            P(("group", "ctx", "head"), None),
            P(("ctx", "head"), None, None),
            P(("ctx", "head"), None, None),
            P(("ctx", "head"), None, None),
        ),
        out_specs=(P(("group", "ctx", "head"), None), P(("group", "ctx", "head"), None)),
        check_vma=False,
    )
```
